32 devices in a mesh: occ: 8 (over z, x), aux: 4 (over y, core).
Axes of the slice: x: 2, y: 2, z: 4, core: 2. Of those that a mesh axis runs over, the one named last changes fastest.
Arguments:
- three_index: bfloat16 [8, 448, 1536], P('occ', None, 'aux'), may hold values from -0.75 to 0.75
- occ_energy: float32 [8], P('occ'), may hold values from -2 to -0.3
- vir_energy: float32 [448], replicated, may hold values from 0.3 to 3
Outputs:
- gamma: float32 [8, 448, 1536], P('occ', None, 'aux')
The draws below stay inside these ranges and needn't reach their ends.
All inputs are finite; a program needn't handle non-finite values.
Results may differ from the reference program's by a relative error of at most 0.0019.
Values may be sent and summed in bfloat16 or wider, within the bound.
A program may use at most 64 MiB of HBM per device.

```python
import jax
import jax.numpy as jnp
from jax import lax

NVIR = 448
NOCC = 8
NAUX = 1536


def steps_of(rng, extent, cuts, least, top_value):
    level = 1.0
    for axis_at, parts in cuts:
        steps = jax.random.uniform(jax.random.fold_in(jax.random.fold_in(rng, 6), axis_at), (parts,), jnp.float32, least / len(cuts), top_value / len(cuts))
        level = level * jnp.repeat(jnp.exp(steps), extent[axis_at] // parts).reshape((-1,) + (1,) * (len(extent) - 1 - axis_at))
    return level


def noise(stream_key, dims, deviation, most, pieces=(), kind=jnp.bfloat16):
    result = deviation * jax.random.normal(stream_key, dims, jnp.float32)
    if pieces:
        result = result * steps_of(stream_key, dims, pieces, -0.22, 0.18)
    return jnp.clip(result, -most, most).astype(kind)


def setup_inputs(seed: int = 0) -> dict:
    key_of = jax.random.split(jax.random.key(seed), 4)
    return {
        "three_index": noise(key_of[0], (NOCC, NVIR, NAUX), 0.05, 0.75, ((0, 8), (2, 4))),
        "occ_energy": jnp.clip(-2.0 + 1.7 * jax.random.uniform(key_of[1], (NOCC,), jnp.float32) ** steps_of(key_of[1], (NOCC,), ((0, 8),), -0.2, 0.2), -2.0, -0.3),
        "vir_energy": jnp.clip(jax.random.uniform(key_of[2], (NVIR,), jnp.float32, 0.3, 3.0), 0.3, 3.0),
    }


def reference(three_index, occ_energy, vir_energy):
    rows = three_index.reshape(NOCC * NVIR, NAUX)
    pair = lax.dot_general(rows, rows, (((1,), (1,)), ((), ())), preferred_element_type=jnp.float32)
    four = pair.reshape(NOCC, NVIR, NOCC, NVIR)
    swapped = jnp.transpose(four, (0, 3, 2, 1))
    denom = (vir_energy[None, :, None, None] + vir_energy[None, None, None, :]
             - occ_energy[:, None, None, None] - occ_energy[None, None, :, None])
    amps = ((2.0 * four - swapped) / denom).astype(jnp.bfloat16).reshape(NOCC * NVIR, NOCC * NVIR)
    gamma = jnp.dot(amps, rows, preferred_element_type=jnp.float32)
    return gamma.reshape(NOCC, NVIR, NAUX)
```

```python
import functools
import heapq

import jax
import jax.numpy as jnp
from jax import lax
from jax.experimental import pallas as pl
from jax.experimental.pallas import tpu as pltpu
from jax.sharding import PartitionSpec as P

MESH = pl.DeviceIdType.MESH
CORES = 2
GATHER_LIMIT = 24 * 1024 * 1024
PIECES = ((0.25, "yxz"), (0.25, "xyz"), (0.25, "zyx"), (0.25, "zxy"))
RATE = {"x": 46.0, "y": 46.0, "z": 46.0, "c": 500.0}
HOP = {"x": 1700.0, "y": 1700.0, "z": 1700.0, "c": 900.0}


def from_behind(array, axis, by):
    size = lax.axis_size(axis)
    return lax.ppermute(array, axis, [(i, (i + by) % size) for i in range(size)])


def reach(size):
    return {1: size // 2, -1: (size - 1) // 2}


def piece_rows(rows):
    pieces, low = [], 0
    for at, (share, order) in enumerate(PIECES):
        count = int(rows * share) // 16 * 16
        if at == len(PIECES) - 1:
            count = rows - low
        pieces.append((low, count, order))
        low += count
    return pieces


def moves(rel, arrived, order, sizes, flip):
    out = []
    first = 0
    if arrived is not None:
        way = 1 if rel[arrived] > 0 else -1
        if abs(rel[arrived]) < reach(sizes[arrived])[way]:
            out.append((arrived, way))
        first = order.index(arrived) + 1
    for dim in order[first:]:
        for way in (1, -1):
            if reach(sizes[dim])[way] >= 1:
                out.append((dim, way))
    return out


def plan(rows, width, sizes):
    pieces = piece_rows(rows)
    free = {}
    heap, count = [], 0
    for at, (_, _, order) in enumerate(pieces):
        heap.append((0.0, count, at, (0, 0, 0), None, "own"))
        count += 1
    heapq.heapify(heap)
    events = []

    def queue(link, now, size):
        start = max(now, free.get(link, 0.0))
        free[link] = start + size / RATE[link[0]]
        return free[link] + HOP[link[0]]

    while heap:
        now, _, at, rel, arrived, kind = heapq.heappop(heap)
        low, number, order = pieces[at]
        size = number * width * 2
        if kind == "core":
            events.append((now, at, rel, "core", ()))
            continue
        named = dict(zip("xyz", rel))
        onward = moves(named, arrived, order, sizes, None)
        sends = []
        for dim, way in onward:
            when = queue((dim, way), now, size)
            after = dict(named)
            after[dim] += way
            heapq.heappush(heap, (when, count, at, (after["x"], after["y"], after["z"]), dim, "link"))
            count += 1
            sends.append((dim, way))
        when = queue(("c", 1), now, size)
        heapq.heappush(heap, (when, count, at, rel, None, "core"))
        count += 1
        events.append((now, at, rel, kind, tuple(sends)))
    return pieces, events


def gather_kernel(nz, nx, ny, b_ref, e_ref, col_ref, row_ref, out_ref, blocks, energies,
                  send_sem, recv_sem, esend_sem, erecv_sem, own_sem):
    rows, width = b_ref.shape
    occ, aux = lax.axis_index("occ"), lax.axis_index("aux")
    z, x = occ // nx, occ % nx
    y, core = aux // CORES, aux % CORES
    sizes = {"x": nx, "y": ny, "z": nz}
    turn = 1 - 2 * core
    pieces, events = plan(rows, width, sizes)
    nocc = nz * nx

    def device(dx, dy, dz, dc):
        return (
            ((z + turn * dz + nz) % nz) * nx + (x + dx + nx) % nx,
            ((y + dy + ny) % ny) * CORES + (core + dc) % CORES,
        )

    barrier = pltpu.get_barrier_semaphore()
    for step in range(1, nocc):
        pl.semaphore_signal(barrier, inc=1, device_id=((occ + step) % nocc, aux), device_id_type=MESH)
    near = [(occ, (aux // CORES) * CORES + (core + 1) % CORES)]
    for way in (1, -1):
        if reach(ny)[way] >= 1:
            near.append(device(0, way, 0, 0))
    for target in near:
        pl.semaphore_signal(barrier, inc=1, device_id=target, device_id_type=MESH)
    pl.semaphore_wait(barrier, nocc - 1 + len(near))

    def columns(shard_aux):
        return pl.ds(pl.multiple_of(shard_aux * width, width), width)

    def place(at, shard):
        low, number, _ = pieces[at]
        return blocks.at[shard[0], pl.ds(low, number), columns(shard[1])]

    def source(at, shard, own):
        low, number, _ = pieces[at]
        return b_ref.at[pl.ds(low, number)] if own else place(at, shard)

    own_copy = pltpu.make_async_copy(b_ref, blocks.at[occ, :, columns(aux)], own_sem)
    own_copy.start()
    sent = []

    def send(at, shard, own, target):
        copy = pltpu.make_async_remote_copy(
            src_ref=source(at, shard, own), dst_ref=place(at, shard),
            send_sem=send_sem.at[len(sent)], recv_sem=recv_sem.at[at, shard[0], shard[1]],
            device_id=target, device_id_type=MESH,
        )
        copy.start()
        sent.append(copy)

    def arrive(at, shard):
        spot = place(at, shard)
        pltpu.make_async_remote_copy(
            src_ref=spot, dst_ref=spot, send_sem=own_sem, recv_sem=recv_sem.at[at, shard[0], shard[1]],
            device_id=(occ, aux), device_id_type=MESH,
        ).wait_recv()

    left = {}
    ready = []
    for _, at, rel, kind, _ in events:
        key = (rel[0] % nx, rel[2] % nz)
        left[key] = left.get(key, 0) + 1
    waiting = {"energies": True}
    small = []
    done = [False]

    def compute(key):
        block = device(-key[0], 0, -key[1], 0)[0]
        mine, other = blocks.at[occ], blocks.at[block]
        value = lax.dot_general(mine[...], other[...], (((1,), (1,)), ((), ())), preferred_element_type=jnp.float32)
        numer = 2.0 * value - value.T
        denom = col_ref[...] + row_ref[...] - e_ref[0:1, 0:1] - energies[block, 0:1, 0:1]
        amps = (numer / denom).astype(jnp.bfloat16)
        term = jnp.dot(amps, blocks[block, :, columns(aux)], preferred_element_type=jnp.float32)
        out_ref[...] = out_ref[...] + term if done[0] else term
        done[0] = True

    started = False
    for _, at, rel, kind, sends in events:
        dx, dy, dz = -rel[0], -rel[1], -rel[2]
        key = (rel[0] % nx, rel[2] % nz)
        if kind == "core":
            arrive(at, partner_shard(device, nz, nx, z, x, y, core, turn, dx, dy, dz, ny))
            rel_key = (rel[0] % nx, (-rel[2]) % nz)
            key = rel_key
        else:
            shard = device(dx, dy, dz, 0)
            if kind == "link":
                arrive(at, shard)
            for dim, way in sends:
                step = {"x": 0, "y": 0, "z": 0}
                step[dim] = way
                send(at, shard, kind == "own", device(step["x"], step["y"], step["z"], 0))
            send(at, shard, kind == "own", device(0, 0, 0, 1))
        left[key] -= 1
        if kind == "own" and not started and at == len(pieces) - 1:
            started = True
            keep = pltpu.make_async_copy(e_ref, energies.at[occ], esend_sem.at[0])
            keep.start()
            for step in range(1, nocc):
                copy = pltpu.make_async_remote_copy(
                    src_ref=e_ref, dst_ref=energies.at[occ], send_sem=esend_sem.at[step],
                    recv_sem=erecv_sem.at[occ], device_id=((occ + step) % nocc, aux), device_id_type=MESH,
                )
                copy.start()
                small.append(copy)
            keep.wait()
            own_copy.wait()
        if left[key] == 0:
            left[key] = -1
            ready.append(key)
            if (0, 0) in ready or done[0]:
                for one in ready:
                    if one != (0, 0) and waiting["energies"]:
                        waiting["energies"] = False
                        for step in range(1, nocc):
                            who = (occ + step) % nocc
                            pltpu.make_async_remote_copy(
                                src_ref=e_ref, dst_ref=energies.at[who], send_sem=own_sem,
                                recv_sem=erecv_sem.at[who], device_id=(occ, aux), device_id_type=MESH,
                            ).wait_recv()
                    compute(one)
                ready.clear()
    for copy in sent + small:
        copy.wait_send()


def partner_shard(device, nz, nx, z, x, y, core, turn, dx, dy, dz, ny):
    return (
        ((z - turn * dz + nz) % nz) * nx + (x + dx + nx) % nx,
        ((y + dy + ny) % ny) * CORES + (core + 1) % CORES,
    )


def gathered(three_index, occ_energy, vir_energy, nz, nx, ny):
    _, rows, width = three_index.shape
    nocc, naux = nz * nx, ny * CORES
    pieces, events = plan(rows, width, {"x": nx, "y": ny, "z": nz})
    copies = sum(len(e[4]) + 1 for e in events if e[3] != "core")
    energy = jnp.broadcast_to(occ_energy.reshape(1, 1), (8, 128))
    vmem = pl.BlockSpec(memory_space=pltpu.VMEM)
    out = pl.pallas_call(
        functools.partial(gather_kernel, nz, nx, ny),
        out_shape=jax.ShapeDtypeStruct((rows, width), jnp.float32),
        in_specs=[vmem] * 4,
        out_specs=vmem,
        scratch_shapes=[
            pltpu.VMEM((nocc, rows, naux * width), three_index.dtype),
            pltpu.VMEM((nocc, 8, 128), jnp.float32),
            pltpu.SemaphoreType.DMA((copies,)),
            pltpu.SemaphoreType.DMA((len(pieces), nocc, naux)),
            pltpu.SemaphoreType.DMA((nocc,)),
            pltpu.SemaphoreType.DMA((nocc,)),
            pltpu.SemaphoreType.DMA,
        ],
        compiler_params=pltpu.CompilerParams(
            collective_id=0, has_side_effects=True, vmem_limit_bytes=48 * 1024 * 1024
        ),
    )(three_index[0], energy, vir_energy[:, None], vir_energy[None, :])
    return out[None]


def pair_amps(rows_i, eps_i, rows_j, eps_j, vir_energy):
    partial_value = lax.dot_general(
        rows_i, rows_j, (((1,), (1,)), ((), ())), preferred_element_type=jnp.float32
    )
    occ_count = eps_i.shape[0]
    vir_count = vir_energy.shape[0]
    width = occ_count * vir_count
    four = partial_value.reshape(occ_count, vir_count, occ_count, vir_count)
    numer = (2.0 * four - jnp.transpose(four, (0, 3, 2, 1))).reshape(width, width)
    denom = (
        vir_energy[None, :, None, None]
        + vir_energy[None, None, None, :]
        - eps_i[:, None, None, None]
        - eps_j[None, None, :, None]
    ).reshape(width, width)
    share = width // lax.axis_size("aux")
    mine = lax.psum_scatter(numer, "aux", scatter_dimension=0, tiled=True)
    lower = lax.axis_index("aux") * share
    denom_rows = lax.dynamic_slice_in_dim(denom, lower, share, 0)
    amps_rows = (mine / denom_rows).astype(jnp.bfloat16)
    amps = lax.all_gather(amps_rows, "aux", axis=0, tiled=True)
    return amps


def apply_other(amps, rows_i):
    return lax.dot_general(
        amps, rows_i, (((0,), (0,)), ((), ())), preferred_element_type=jnp.float32
    )


def local(three_index, occ_energy, vir_energy):
    occ_count, vir_count, aux_count = three_index.shape
    cycle_size = lax.axis_size("occ")
    my_index = lax.axis_index("occ")
    all_energy = lax.all_gather(occ_energy, "occ", axis=0, tiled=True)
    own_rows = three_index.reshape(occ_count * vir_count, aux_count)

    def energy_of(step):
        block = (my_index - step + cycle_size) % cycle_size
        return lax.dynamic_slice_in_dim(all_energy, block * occ_count, occ_count)

    amps = pair_amps(own_rows, occ_energy, own_rows, occ_energy, vir_energy)
    gamma = jnp.dot(amps, own_rows, preferred_element_type=jnp.float32)
    half = cycle_size // 2
    carried = jnp.zeros_like(gamma)

    def cycle_step(step, state):
        rows_j, carried, gamma = state
        rows_j = from_behind(rows_j, "occ", 1)
        carried = from_behind(carried, "occ", 1)
        amps = pair_amps(own_rows, occ_energy, rows_j, energy_of(step), vir_energy)
        gamma = gamma + jnp.dot(amps, rows_j, preferred_element_type=jnp.float32)
        carried = carried + apply_other(amps, own_rows)
        return (rows_j, carried, gamma)

    rows_j, carried, gamma = lax.fori_loop(1, half, cycle_step, (own_rows, carried, gamma))
    rows_j = from_behind(rows_j, "occ", 1)
    amps = pair_amps(own_rows, occ_energy, rows_j, energy_of(half), vir_energy)
    gamma = gamma + jnp.dot(amps, rows_j, preferred_element_type=jnp.float32)
    returned = from_behind(carried, "occ", 1 - half)
    gamma = gamma + returned
    return gamma.reshape(occ_count, vir_count, aux_count)


def solution(mesh):
    nocc, naux = mesh.shape["occ"], mesh.shape["aux"]

    def either(three_index, occ_energy, vir_energy):
        _, rows, width = three_index.shape
        whole = nocc * naux * three_index.size * three_index.dtype.itemsize
        fits = whole <= GATHER_LIMIT and three_index.shape[0] == 1
        if fits and naux % CORES == 0 and nocc % 2 == 0:
            return gathered(three_index, occ_energy, vir_energy, nocc // 2, 2, naux // CORES)
        return local(three_index, occ_energy, vir_energy)

    return jax.shard_map(
        either,
        mesh=mesh,
        in_specs=(P("occ", None, "aux"), P("occ"), P()),
        out_specs=P("occ", None, "aux"),
        check_vma=False,
    )
```

```python
import functools
import heapq
import itertools

import jax
import jax.numpy as jnp
from jax import lax
from jax.experimental import pallas as pl
from jax.experimental.pallas import tpu as pltpu
from jax.sharding import PartitionSpec as P

MESH = pl.DeviceIdType.MESH
CORES = 2
GATHER_LIMIT = 24 * 1024 * 1024
LANES = 128
RATE = 46250.0
HOP = 2.4
AHEAD = 2.0
SLACK = 0.0
RETURN = 5.3
LAST = 50
MIRROR = 1.0
MATMUL = 0.45
ELEMENT = 0.25
APPLY = 0.35
EXCHANGE = 1.5
STEP = {"x": (1, 0, 0), "y": (0, 1, 0), "+": (0, 0, 1), "-": (0, 0, -1)}
BACK = {"x": "x", "y": "y", "+": "-", "-": "+"}
ROUTES = (
    (".xyxy+++x++y....", ".xyy+++x+xyx....", ".xyx+++++xy+....", ".xyx+-+++xyy...."),
    ("-yx-.xyx++yx+xyx", "-yyx.xxy+xy-x+xy", "y--y.xyy++-++xyy", "---x.yyx+x++yyx+"),
)
URGENCY = (4, -1, 0, 0, -2, -4, 0, 1)
DEPTH = 0.5


def from_behind(array, axis, by):
    size = lax.axis_size(axis)
    return lax.ppermute(array, axis, [(i, (i + by) % size) for i in range(size)])


def moved(chip, link):
    dx, dy, dz = STEP[link]
    return ((chip[0] + dx) % 2, (chip[1] + dy) % 2, chip[2] + dz)


def piece_rows(rows):
    number = len(ROUTES[0])
    tiles = rows // 16
    lows = [16 * (tiles * at // number) for at in range(number)] + [rows]
    return [(lows[at], lows[at + 1] - lows[at]) for at in range(number)]


def routes():
    out = []
    for a, b, mirrored in itertools.product(range(2), repeat=3):
        for plane in range(2):
            for piece, text in enumerate(ROUTES[plane]):
                tree = {}
                for z, y, x in itertools.product(range(4), range(2), range(2)):
                    link = text[x + 2 * y + 4 * z]
                    if link == ".":
                        continue
                    px, py, pz = moved((x, y, z), BACK[link])
                    parent = (px ^ a, py ^ b, 3 - pz if mirrored else pz)
                    tree.setdefault(parent, []).append(BACK[link] if mirrored and link in "+-" else link)
                out.append(((a, b, 3 - plane if mirrored else plane), piece, tree))
    return out


def depth_of(tree, chip, known):
    if chip not in known:
        known[chip] = 1 + max([depth_of(tree, moved(chip, link), known) for link in tree.get(chip, ())] or [-1])
    return known[chip]


def timeline(pieces, width):
    items = routes()
    known = [{} for _ in items]
    waiting, busy, arrivals, order, heap = {}, set(), {}, {}, []
    plain = len(items)
    missing = {(x, y, z): 4 * len(pieces) for x, y, z in itertools.product(range(2), range(2), (1, 2))}
    count = itertools.count()
    for at, (source, _, _) in enumerate(items):
        heapq.heappush(heap, (0.0, next(count), True, at, source))

    def start(lane, now):
        if lane in busy or not waiting.get(lane):
            return
        _, _, at, target = heapq.heappop(waiting[lane])
        busy.add(lane)
        taken = pieces[items[at][1]][1] * width * 2 / RATE
        order.setdefault(lane, []).append((now, at))
        heapq.heappush(heap, (now + taken, next(count), False, lane, None))
        heapq.heappush(heap, (now + taken + HOP, next(count), True, at, target))

    while heap:
        now, _, arrived, at, chip = heapq.heappop(heap)
        if not arrived:
            busy.discard(at)
            start(at, now)
            continue
        source, _, tree = items[at]
        arrivals[at, chip] = now
        if at < plain and chip in missing and source[2] == (3 if chip[2] == 1 else 0):
            missing[chip] -= 1
            if missing[chip] == 0:
                for piece in range(len(pieces)):
                    items.append((chip, piece, {chip: ["-" if chip[2] == 1 else "+"]}))
                    known.append({})
                    heapq.heappush(heap, (now + RETURN, next(count), True, len(items) - 1, chip))
        for link in tree.get(chip, ()):
            target = moved(chip, link)
            plane, goal = source[2], target[2]
            if goal >= 2:
                plane, goal = 3 - plane, 3 - goal
            rank = -DEPTH * depth_of(tree, target, known[at]) - URGENCY[2 * plane + goal] if at < plain else LAST
            heapq.heappush(waiting.setdefault((chip, link), []), (rank, next(count), at, target))
            start((chip, link), now)
    return items, arrivals, order, plain


def compute_steps(ready, inner):
    own = 1 if inner else 0
    tasks = []
    for plane, when in ready.items():
        if inner and plane == 3:
            tasks.append((max(when, ready[0]), 0, plane, True))
        tasks.append((max(when, ready[own]), 1, plane, False))
    tasks.sort()
    steps, clock, later = [], 0.0, []
    halves, parts = 2, 4

    def settle(now):
        nonlocal clock
        while later and later[0][0] <= now:
            when, at = heapq.heappop(later)
            clock = max(clock, when)
            steps.append((clock, "other", at, 0))
            clock += APPLY
            if tasks[at][3]:
                steps.append((clock, "return", at, 0))

    for at, (when, _, plane, far) in enumerate(tasks):
        settle(max(clock, when))
        clock = max(clock, when)
        steps.append((clock, "open", at, 0))
        for part in range(halves):
            settle(clock)
            steps.append((clock, "matmul", at, part))
            clock += MATMUL
        for part in range(parts):
            settle(clock)
            steps.append((clock, "element", at, part))
            clock += ELEMENT
        steps.append((clock, "mine", at, 0))
        clock += APPLY
        heapq.heappush(later, (clock + EXCHANGE, at))
    settle(1e9)
    return [(plane, far) for _, _, plane, far in tasks], steps, clock


def program_of(plane, pieces, width):
    items, arrivals, order, plain = timeline(pieces, width)
    chip = (0, 0, plane)
    events = []
    ready = {}
    for at, (source, piece, _) in enumerate(items[:plain]):
        if (at, chip) in arrivals:
            ready[source[2]] = max(ready.get(source[2], 0.0), arrivals[at, chip] + MIRROR)
    tasks, steps, end = compute_steps(ready, plane == 1)
    back = max([when for when, kind, _, _ in steps if kind == "return"] or [0.0])
    first = {}
    for link in STEP:
        last = 0.0
        for when, at in order.get((chip, link), ()):
            last = max(last, arrivals[at, chip], when - AHEAD)
            if at < plain:
                first[at] = min(first.get(at, 1e9), last)
                events.append((last, 2, ("send", items[at][0], items[at][1], link)))
            else:
                events.append((max(last, back + 0.01), 4, ("return", items[at][1])))
    for at, (source, piece, _) in enumerate(items[:plain]):
        if (at, chip) in arrivals:
            when = min(arrivals[at, chip] + SLACK, first.get(at, 1e9))
            events.append((when, 1, ("take", source, piece)))
    events += [(when, 3, ("step", *step)) for when, *step in steps]
    for away in range(4 if plane == 1 else 3):
        if away != plane:
            events.append((5.0 * abs(away - plane), 0, ("energy", away)))
    if plane == 0:
        events.append((end + 100.0, 4, ("far",)))
    events.sort(key=lambda event: event[:2])
    return [event[2] for event in events], tasks


def gather_kernel(nz, nx, ny, b_ref, e_ref, col_ref, row_ref, out_ref, blocks, energies, value, mine_amps, other_amps,
                  total, leave, come, send_sem, recv_sem, msend_sem, mrecv_sem, esend_sem, erecv_sem,
                  asend_sem, arecv_sem, fsend_sem, frecv_sem, unused_sem):
    rows, width = b_ref.shape
    occ, aux = lax.axis_index("occ"), lax.axis_index("aux")
    z, x = occ // nx, occ % nx
    y, core = aux // CORES, aux % CORES
    upper = z // 2
    plane = z + upper * (nz - 1 - 2 * z)
    pieces = piece_rows(rows)

    def plane_at(k):
        return k + upper * (nz - 1 - 2 * k)

    def block_at(dx, k):
        return plane_at(k) * nx + (x + dx) % nx

    def device(dx, dy, k, dc=0):
        return block_at(dx, k), ((y + dy) % ny) * CORES + (core + dc) % CORES

    def neighbour(me, link):
        dx, dy, dz = STEP[link]
        return device(dx, dy, me + dz)

    partner = (occ, y * CORES + (core + 1) % CORES)
    barrier = pltpu.get_barrier_semaphore()
    step_up = 1 - 2 * upper
    near = [
        partner,
        (z * nx + (x + 1) % nx, aux),
        (occ, ((y + 1) % ny) * CORES + core),
        ((z + step_up) * nx + x, aux),
    ]
    for target in near:
        pl.semaphore_signal(barrier, inc=1, device_id=target, device_id_type=MESH)

    @pl.when(plane == 1)
    def _():
        pl.semaphore_signal(barrier, inc=1, device_id=((z - step_up) * nx + x, aux), device_id_type=MESH)

    pl.semaphore_wait(barrier, len(near) + plane)

    def columns(shard_aux):
        return pl.ds(pl.multiple_of(shard_aux * width, width), width)

    def run(me):
        events, tasks = program_of(me, pieces, width)
        sent = []
        taken = set()
        started = {}

        def place(source, piece, dc=0):
            block, shard_aux = device(source[0], source[1], source[2], dc)
            low, number = pieces[piece]
            return blocks.at[block, pl.ds(low, number), columns(shard_aux)]

        def chip_index(source):
            block, shard_aux = device(*source)
            return block * ny + shard_aux // CORES

        def origin(source, piece):
            low, number = pieces[piece]
            return b_ref.at[pl.ds(low, number)] if source == (0, 0, me) else place(source, piece)

        def remote(src, dst, send, recv, target):
            return pltpu.make_async_remote_copy(
                src_ref=src, dst_ref=dst, send_sem=send, recv_sem=recv, device_id=target, device_id_type=MESH
            )

        def start(copy):
            copy.start()
            sent.append(copy)

        def arrived(spot, sem):
            remote(spot, spot, unused_sem, sem, (occ, aux)).wait_recv()

        for target in ["x", "+"] + (["-"] if me == 1 else []):
            start(remote(e_ref, energies.at[occ], esend_sem.at[len(sent)], erecv_sem.at[occ], neighbour(me, target)))
        number_sent = [0]

        def send(source, piece, link):
            copy = remote(
                origin(source, piece), place(source, piece), send_sem.at[number_sent[0]],
                recv_sem.at[piece, chip_index(source)], neighbour(me, link),
            )
            number_sent[0] += 1
            start(copy)

        def take(source, piece):
            if source != (0, 0, me):
                arrived(place(source, piece), recv_sem.at[piece, chip_index(source)])
            start(remote(
                origin(source, piece), place(source, piece), msend_sem.at[piece, chip_index(source)],
                mrecv_sem.at[piece, chip_index(source)], partner,
            ))

        def pass_energy(away):
            if away in passed:
                return
            passed.add(away)
            block = block_at(0, away)
            arrived(energies.at[block], erecv_sem.at[block])
            onward = ["x"] + ({0: ["+"], 2: ["-"]}.get(away, []) if me == 1 else [])
            for link in onward:
                start(remote(energies.at[block], energies.at[block], esend_sem.at[count_energy[0]],
                             erecv_sem.at[block], neighbour(me, link)))
                count_energy[0] += 1

        count_energy = [len(sent)]
        passed = {me}
        blocks[occ, :, columns(aux)] = b_ref[...]
        energies[occ] = e_ref[...]

        def open_plane(k):
            if k in taken:
                return
            taken.add(k)
            pass_energy(k)
            for source in itertools.product(range(2), range(2), [k]):
                for piece in range(len(pieces)):
                    arrived(place(source, piece, 1), mrecv_sem.at[piece, chip_index(source)])
            block = block_at(1, k)
            arrived(energies.at[block], erecv_sem.at[block])

        def apply(amps, block, far, fresh):
            term = jnp.dot(amps, blocks[block, :, columns(aux)], preferred_element_type=jnp.float32)
            goal = total if far else out_ref
            goal[...] = term if fresh else goal[...] + term

        def step(kind, at, part):
            k, far = tasks[at]
            left = block_at(0, 0) if far else occ
            right = plane_at(k) * nx + (x + core) % nx
            if kind == "open":
                open_plane(0 if far else me)
                open_plane(k)
            elif kind == "matmul":
                cut = rows // 2 // LANES * LANES + LANES if rows > LANES else rows
                low, high = ((0, min(cut, rows)), (min(cut, rows), rows))[part]
                if high > low:
                    value[:, low:high] = lax.dot_general(
                        blocks[left], blocks[right, low:high, :], (((1,), (1,)), ((), ())),
                        preferred_element_type=jnp.float32,
                    )
            elif kind == "element":
                size = -(-rows // (4 * LANES)) * LANES
                low, high = min(part * size, rows), min(part * size + size, rows)
                if high > low:
                    numer = 2.0 * value[low:high, :] - value[:, low:high].T
                    denom = col_ref[low:high, :] + row_ref[...] - energies[left, 0:1, 0:1] - energies[right, 0:1, 0:1]
                    mine_amps[at, low:high, :] = (numer / denom).astype(jnp.bfloat16)
            elif kind == "mine":
                apply(mine_amps[at], right, far, far not in started)
                started[far] = True
                start(remote(mine_amps.at[at], other_amps.at[at], asend_sem.at[at], arecv_sem.at[at], partner))
            elif kind == "other":
                arrived(other_amps.at[at], arecv_sem.at[at])
                apply(other_amps[at], plane_at(k) * nx + (x + 1 - core) % nx, far, False)
            elif kind == "return":
                leave[...] = total[...].astype(jnp.bfloat16)

        for event in events:
            if event[0] == "take":
                take(*event[1:])
            elif event[0] == "send":
                send(*event[1:])
            elif event[0] == "energy":
                pass_energy(event[1])
            elif event[0] == "step":
                step(*event[1:])
            elif event[0] == "return":
                spot = pl.ds(*pieces[event[1]])
                start(remote(leave.at[spot], come.at[spot], fsend_sem.at[event[1]], frecv_sem.at[event[1]],
                             neighbour(me, "-")))
            else:
                for piece, (low, number) in enumerate(pieces):
                    spot = slice(low, low + number)
                    arrived(come.at[pl.ds(low, number)], frecv_sem.at[piece])
                    out_ref[spot, :] = out_ref[spot, :] + come[spot, :].astype(jnp.float32)
        for copy in sent:
            copy.wait_send()

    @pl.when(plane == 0)
    def _():
        run(0)

    @pl.when(plane == 1)
    def _():
        run(1)


def gathered(three_index, occ_energy, vir_energy, nz, nx, ny):
    _, rows, width = three_index.shape
    nocc, naux = nz * nx, ny * CORES
    pieces = piece_rows(rows)
    copies = max(sum(event[0] == "send" for event in program_of(plane, pieces, width)[0]) for plane in range(2))
    tasks = 5
    energy = jnp.broadcast_to(occ_energy.reshape(1, 1), (8, LANES))
    vmem = pl.BlockSpec(memory_space=pltpu.VMEM)
    dma = pltpu.SemaphoreType.DMA
    kind = three_index.dtype
    out = pl.pallas_call(
        functools.partial(gather_kernel, nz, nx, ny),
        out_shape=jax.ShapeDtypeStruct((rows, width), jnp.float32),
        in_specs=[vmem] * 4,
        out_specs=vmem,
        scratch_shapes=[
            pltpu.VMEM((nocc, rows, naux * width), kind),
            pltpu.VMEM((nocc, 8, LANES), jnp.float32),
            pltpu.VMEM((rows, rows), jnp.float32),
            pltpu.VMEM((tasks, rows, rows), jnp.bfloat16),
            pltpu.VMEM((tasks, rows, rows), jnp.bfloat16),
            pltpu.VMEM((rows, width), jnp.float32),
            pltpu.VMEM((rows, width), jnp.bfloat16),
            pltpu.VMEM((rows, width), jnp.bfloat16),
            dma((copies,)),
            dma((len(pieces), nocc * ny)),
            dma((len(pieces), nocc * ny)),
            dma((len(pieces), nocc * ny)),
            dma((16,)),
            dma((nocc,)),
            dma((tasks,)),
            dma((tasks,)),
            dma((len(pieces),)),
            dma((len(pieces),)),
            dma,
        ],
        compiler_params=pltpu.CompilerParams(
            collective_id=0, has_side_effects=True, vmem_limit_bytes=48 * 1024 * 1024
        ),
    )(three_index[0], energy, vir_energy[:, None], vir_energy[None, :])
    return out[None]


def pair_amps(rows_i, eps_i, rows_j, eps_j, vir_energy):
    partial_value = lax.dot_general(
        rows_i, rows_j, (((1,), (1,)), ((), ())), preferred_element_type=jnp.float32
    )
    occ_count = eps_i.shape[0]
    vir_count = vir_energy.shape[0]
    width = occ_count * vir_count
    four = partial_value.reshape(occ_count, vir_count, occ_count, vir_count)
    numer = (2.0 * four - jnp.transpose(four, (0, 3, 2, 1))).reshape(width, width)
    denom = (
        vir_energy[None, :, None, None]
        + vir_energy[None, None, None, :]
        - eps_i[:, None, None, None]
        - eps_j[None, None, :, None]
    ).reshape(width, width)
    share = width // lax.axis_size("aux")
    mine = lax.psum_scatter(numer, "aux", scatter_dimension=0, tiled=True)
    lower = lax.axis_index("aux") * share
    denom_rows = lax.dynamic_slice_in_dim(denom, lower, share, 0)
    amps_rows = (mine / denom_rows).astype(jnp.bfloat16)
    amps = lax.all_gather(amps_rows, "aux", axis=0, tiled=True)
    return amps


def apply_other(amps, rows_i):
    return lax.dot_general(
        amps, rows_i, (((0,), (0,)), ((), ())), preferred_element_type=jnp.float32
    )


def local(three_index, occ_energy, vir_energy):
    occ_count, vir_count, aux_count = three_index.shape
    cycle_size = lax.axis_size("occ")
    my_index = lax.axis_index("occ")
    all_energy = lax.all_gather(occ_energy, "occ", axis=0, tiled=True)
    own_rows = three_index.reshape(occ_count * vir_count, aux_count)

    def energy_of(step):
        block = (my_index - step + cycle_size) % cycle_size
        return lax.dynamic_slice_in_dim(all_energy, block * occ_count, occ_count)

    amps = pair_amps(own_rows, occ_energy, own_rows, occ_energy, vir_energy)
    gamma = jnp.dot(amps, own_rows, preferred_element_type=jnp.float32)
    half = cycle_size // 2
    carried = jnp.zeros_like(gamma)

    def cycle_step(step, state):
        rows_j, carried, gamma = state
        rows_j = from_behind(rows_j, "occ", 1)
        carried = from_behind(carried, "occ", 1)
        amps = pair_amps(own_rows, occ_energy, rows_j, energy_of(step), vir_energy)
        gamma = gamma + jnp.dot(amps, rows_j, preferred_element_type=jnp.float32)
        carried = carried + apply_other(amps, own_rows)
        return (rows_j, carried, gamma)

    rows_j, carried, gamma = lax.fori_loop(1, half, cycle_step, (own_rows, carried, gamma))
    rows_j = from_behind(rows_j, "occ", 1)
    amps = pair_amps(own_rows, occ_energy, rows_j, energy_of(half), vir_energy)
    gamma = gamma + jnp.dot(amps, rows_j, preferred_element_type=jnp.float32)
    returned = from_behind(carried, "occ", 1 - half)
    gamma = gamma + returned
    return gamma.reshape(occ_count, vir_count, aux_count)


def solution(mesh):
    nocc, naux = mesh.shape["occ"], mesh.shape["aux"]

    def either(three_index, occ_energy, vir_energy):
        _, rows, width = three_index.shape
        whole = nocc * naux * three_index.size * three_index.dtype.itemsize
        pieces = len(ROUTES[0])
        fits = whole <= GATHER_LIMIT and three_index.shape[0] == 1
        fits = fits and rows % 16 == 0 and rows // 16 >= pieces and width % LANES == 0
        if fits and nocc == 8 and naux == 2 * CORES:
            return gathered(three_index, occ_energy, vir_energy, nocc // 2, 2, naux // CORES)
        return local(three_index, occ_energy, vir_energy)

    return jax.shard_map(
        either,
        mesh=mesh,
        in_specs=(P("occ", None, "aux"), P("occ"), P()),
        out_specs=P("occ", None, "aux"),
        check_vma=False,
    )
```

```python
import functools
import heapq
import itertools

import jax
import jax.numpy as jnp
from jax import lax
from jax.experimental import pallas as pl
from jax.experimental.pallas import tpu as pltpu
from jax.sharding import PartitionSpec as P

MESH = pl.DeviceIdType.MESH
CORES = 2
GATHER_LIMIT = 24 * 1024 * 1024
LANES = 128
RATE = 46250.0
HOP = 2.4
AHEAD = 2.0
SLACK = 0.0
RETURN = 5.0
LAST = 0
MIRROR = 1.0
MATMUL = 0.45
ELEMENT = 0.25
APPLY = 0.35
EXCHANGE = 1.5
STEP = {"x": (1, 0, 0), "y": (0, 1, 0), "+": (0, 0, 1), "-": (0, 0, -1)}
BACK = {"x": "x", "y": "y", "+": "-", "-": "+"}
ROUTES = (
    (".xyx+x+++xyy....", ".xyx+++-+++x....", ".xyx+xy++xyy....", ".xyy+-y++xy+...."),
    ("--yy.x+++xyyyy+x", "--yx.xyxx++-++xy", "yx-x.xy++xy-+x+y", "--yx.xyy+xy++xyx"),
)
URGENCY = (4, 1, -1, -2, -1, -2, -1, -1)
DEPTH = 0.5


def from_behind(array, axis, by):
    size = lax.axis_size(axis)
    return lax.ppermute(array, axis, [(i, (i + by) % size) for i in range(size)])


def moved(chip, link):
    dx, dy, dz = STEP[link]
    return ((chip[0] + dx) % 2, (chip[1] + dy) % 2, chip[2] + dz)


def piece_rows(rows):
    number = len(ROUTES[0])
    tiles = rows // 16
    lows = [16 * (tiles * at // number) for at in range(number)] + [rows]
    return [(lows[at], lows[at + 1] - lows[at]) for at in range(number)]


def routes():
    out = []
    for a, b, mirrored in itertools.product(range(2), repeat=3):
        for plane in range(2):
            for piece, text in enumerate(ROUTES[plane]):
                tree = {}
                for z, y, x in itertools.product(range(4), range(2), range(2)):
                    link = text[x + 2 * y + 4 * z]
                    if link == ".":
                        continue
                    px, py, pz = moved((x, y, z), BACK[link])
                    parent = (px ^ a, py ^ b, 3 - pz if mirrored else pz)
                    tree.setdefault(parent, []).append(BACK[link] if mirrored and link in "+-" else link)
                out.append(((a, b, 3 - plane if mirrored else plane), piece, tree))
    return out


def depth_of(tree, chip, known):
    if chip not in known:
        known[chip] = 1 + max([depth_of(tree, moved(chip, link), known) for link in tree.get(chip, ())] or [-1])
    return known[chip]


def timeline(pieces, width):
    items = routes()
    known = [{} for _ in items]
    waiting, busy, arrivals, order, heap = {}, set(), {}, {}, []
    plain = len(items)
    missing = {(x, y, z): 6 * len(pieces) for x, y, z in itertools.product(range(2), range(2), (1, 2))}
    count = itertools.count()
    for at, (source, _, _) in enumerate(items):
        heapq.heappush(heap, (0.0, next(count), True, at, source))

    def start(lane, now):
        if lane in busy or not waiting.get(lane):
            return
        _, _, at, target = heapq.heappop(waiting[lane])
        busy.add(lane)
        taken = pieces[items[at][1]][1] * width * 2 / RATE
        order.setdefault(lane, []).append((now, at))
        heapq.heappush(heap, (now + taken, next(count), False, lane, None))
        heapq.heappush(heap, (now + taken + HOP, next(count), True, at, target))

    while heap:
        now, _, arrived, at, chip = heapq.heappop(heap)
        if not arrived:
            busy.discard(at)
            start(at, now)
            continue
        source, _, tree = items[at]
        arrivals[at, chip] = now
        if at < plain and chip in missing:
            far, near = (3, 0) if chip[2] == 1 else (0, 3)
            if source[2] == far or source[::2] == (chip[0], near):
                missing[chip] -= 1
                ended = missing[chip] == 0
            else:
                ended = False
            if ended:
                for piece in range(len(pieces)):
                    items.append((chip, piece, {chip: ["-" if chip[2] == 1 else "+"]}))
                    known.append({})
                    heapq.heappush(heap, (now + RETURN, next(count), True, len(items) - 1, chip))
        for link in tree.get(chip, ()):
            target = moved(chip, link)
            plane, goal = source[2], target[2]
            if goal >= 2:
                plane, goal = 3 - plane, 3 - goal
            rank = -DEPTH * depth_of(tree, target, known[at]) - URGENCY[2 * plane + goal] if at < plain else LAST
            heapq.heappush(waiting.setdefault((chip, link), []), (rank, next(count), at, target))
            start((chip, link), now)
    return items, arrivals, order, plain


def compute_steps(ready, inner):
    own = 1 if inner else 0
    tasks, jobs = [], []
    work = [("open", 0, 0.0)] + [("matmul", part, MATMUL) for part in range(2)]
    work += [("element", part, ELEMENT) for part in range(4)] + [("mine", 0, APPLY)]
    for plane in sorted({key[0] for key in ready}):
        both = max(ready[plane, 0], ready[plane, 1])
        if inner and plane == 3:
            jobs.append((max(both, ready[0, 0]), 0, len(tasks), list(work)))
            tasks.append((plane, True))
        jobs.append((max(both, ready[own, 0]), 2, len(tasks), list(work)))
        tasks.append((plane, False))
    steps, clock = [], 0.0
    while jobs:
        clock = max(clock, min(job[0] for job in jobs))
        job = min((job for job in jobs if job[0] <= clock), key=lambda job: (job[1], job[0], job[2]))
        kind, part, cost = job[3].pop(0)
        steps.append((clock, kind, job[2], part))
        clock += cost
        if not job[3]:
            jobs.remove(job)
        if kind == "mine":
            rest = [("other", 0, APPLY)] + ([("return", 0, 0.1)] if tasks[job[2]][1] else [])
            jobs.append((clock + EXCHANGE, min(job[1], 1), job[2], rest))
    return tasks, steps, clock


def program_of(plane, pieces, width):
    items, arrivals, order, plain = timeline(pieces, width)
    chip = (0, 0, plane)
    events = []
    ready = {}
    for at, (source, piece, _) in enumerate(items[:plain]):
        if (at, chip) in arrivals:
            key = (source[2], source[0])
            ready[key] = max(ready.get(key, 0.0), arrivals[at, chip] + MIRROR)
    tasks, steps, end = compute_steps(ready, plane == 1)
    back = max([when for when, kind, _, _ in steps if kind == "return"] or [0.0])
    first = {}
    for link in STEP:
        last = 0.0
        for when, at in order.get((chip, link), ()):
            last = max(last, arrivals[at, chip], when - AHEAD)
            if at < plain:
                first[at] = min(first.get(at, 1e9), last)
                events.append((last, 2, ("send", items[at][0], items[at][1], link)))
            else:
                events.append((max(last, back + 0.01), 4, ("return", items[at][1])))
    for at, (source, piece, _) in enumerate(items[:plain]):
        if (at, chip) in arrivals:
            when = min(arrivals[at, chip] + SLACK, first.get(at, 1e9))
            events.append((when, 1, ("take", source, piece)))
    events += [(when, 3, ("step", *step)) for when, *step in steps]
    for away in range(4 if plane == 1 else 3):
        if away != plane:
            events.append((5.0 * abs(away - plane), 0, ("energy", away)))
    if plane == 0:
        events.append((end + 100.0, 4, ("far",)))
    events.sort(key=lambda event: event[:2])
    return [event[2] for event in events], tasks


def gather_kernel(nz, nx, ny, b_ref, e_ref, col_ref, row_ref, out_ref, blocks, energies, value, mine_amps, other_amps,
                  total, leave, come, send_sem, recv_sem, msend_sem, mrecv_sem, esend_sem, erecv_sem,
                  asend_sem, arecv_sem, fsend_sem, frecv_sem, keep_sem, unused_sem):
    rows, width = b_ref.shape
    occ, aux = lax.axis_index("occ"), lax.axis_index("aux")
    z, x = occ // nx, occ % nx
    y, core = aux // CORES, aux % CORES
    upper = z // 2
    plane = z + upper * (nz - 1 - 2 * z)
    pieces = piece_rows(rows)

    def plane_at(k):
        return k + upper * (nz - 1 - 2 * k)

    def block_at(dx, k):
        return plane_at(k) * nx + (x + dx) % nx

    def device(dx, dy, k, dc=0):
        return block_at(dx, k), ((y + dy) % ny) * CORES + (core + dc) % CORES

    def neighbour(me, link):
        dx, dy, dz = STEP[link]
        return device(dx, dy, me + dz)

    def columns(shard_aux):
        return pl.ds(pl.multiple_of(shard_aux * width, width), width)

    keep = pltpu.make_async_copy(b_ref, blocks.at[occ, :, columns(aux)], keep_sem)
    keep.start()
    partner = (occ, y * CORES + (core + 1) % CORES)
    barrier = pltpu.get_barrier_semaphore()
    step_up = 1 - 2 * upper
    near = [
        partner,
        (z * nx + (x + 1) % nx, aux),
        (occ, ((y + 1) % ny) * CORES + core),
        ((z + step_up) * nx + x, aux),
    ]
    for target in near:
        pl.semaphore_signal(barrier, inc=1, device_id=target, device_id_type=MESH)

    @pl.when(plane == 1)
    def _():
        pl.semaphore_signal(barrier, inc=1, device_id=((z - step_up) * nx + x, aux), device_id_type=MESH)

    pl.semaphore_wait(barrier, len(near) + plane)

    def run(me):
        events, tasks = program_of(me, pieces, width)
        sent = []
        taken = set()
        started = {}

        def place(source, piece, dc=0):
            block, shard_aux = device(source[0], source[1], source[2], dc)
            low, number = pieces[piece]
            return blocks.at[block, pl.ds(low, number), columns(shard_aux)]

        def chip_index(source):
            block, shard_aux = device(*source)
            return block * ny + shard_aux // CORES

        def origin(source, piece):
            low, number = pieces[piece]
            return b_ref.at[pl.ds(low, number)] if source == (0, 0, me) else place(source, piece)

        def remote(src, dst, send, recv, target):
            return pltpu.make_async_remote_copy(
                src_ref=src, dst_ref=dst, send_sem=send, recv_sem=recv, device_id=target, device_id_type=MESH
            )

        def start(copy):
            copy.start()
            sent.append(copy)

        def arrived(spot, sem):
            remote(spot, spot, unused_sem, sem, (occ, aux)).wait_recv()

        for target in ["x", "+"] + (["-"] if me == 1 else []):
            start(remote(e_ref, energies.at[occ], esend_sem.at[len(sent)], erecv_sem.at[occ], neighbour(me, target)))
        number_sent = [0]

        def send(source, piece, link):
            copy = remote(
                origin(source, piece), place(source, piece), send_sem.at[number_sent[0]],
                recv_sem.at[piece, chip_index(source)], neighbour(me, link),
            )
            number_sent[0] += 1
            start(copy)

        def take(source, piece):
            if source != (0, 0, me):
                arrived(place(source, piece), recv_sem.at[piece, chip_index(source)])
            start(remote(
                origin(source, piece), place(source, piece), msend_sem.at[piece, chip_index(source)],
                mrecv_sem.at[piece, chip_index(source)], partner,
            ))

        def pass_energy(away):
            if away in passed:
                return
            passed.add(away)
            block = block_at(0, away)
            arrived(energies.at[block], erecv_sem.at[block])
            onward = ["x"] + ({0: ["+"], 2: ["-"]}.get(away, []) if me == 1 else [])
            for link in onward:
                start(remote(energies.at[block], energies.at[block], esend_sem.at[count_energy[0]],
                             erecv_sem.at[block], neighbour(me, link)))
                count_energy[0] += 1

        count_energy = [len(sent)]
        passed = {me}
        energies[occ] = e_ref[...]

        def open_block(dx, k):
            if (dx, k) in taken:
                return
            taken.add((dx, k))
            if dx == 0:
                pass_energy(k)
            else:
                block = block_at(1, k)
                arrived(energies.at[block], erecv_sem.at[block])
            if (dx, k) == (0, me):
                keep.wait()
            for source in itertools.product([dx], range(2), [k]):
                for piece in range(len(pieces)):
                    arrived(place(source, piece, 1), mrecv_sem.at[piece, chip_index(source)])

        def hand_over(at, part):
            size = -(-rows // (4 * LANES)) * LANES
            low, high = min(part * size, rows), min(part * size + size, rows)
            if high > low:
                spot = pl.ds(low, high - low)
                start(remote(mine_amps.at[at, spot], other_amps.at[at, spot], asend_sem.at[at, part],
                             arecv_sem.at[at, part], partner))

        def apply(amps, block, far, fresh):
            term = jnp.dot(amps, blocks[block, :, columns(aux)], preferred_element_type=jnp.float32)
            goal = total if far else out_ref
            goal[...] = term if fresh else goal[...] + term

        def step(kind, at, part):
            k, far = tasks[at]
            left = block_at(0, 0) if far else occ
            right = plane_at(k) * nx + (x + core) % nx
            if kind == "open":
                open_block(0, 0 if far else me)
                open_block(0, k)
                open_block(1, k)
            elif kind == "matmul":
                cut = rows // 2 // LANES * LANES + LANES if rows > LANES else rows
                low, high = ((0, min(cut, rows)), (min(cut, rows), rows))[part]
                if high > low:
                    value[int(far), :, low:high] = lax.dot_general(
                        blocks[left], blocks[right, low:high, :], (((1,), (1,)), ((), ())),
                        preferred_element_type=jnp.float32,
                    )
            elif kind == "element":
                size = -(-rows // (4 * LANES)) * LANES
                low, high = min(part * size, rows), min(part * size + size, rows)
                if high > low:
                    numer = 2.0 * value[int(far), low:high, :] - value[int(far), :, low:high].T
                    denom = col_ref[low:high, :] + row_ref[...] - energies[left, 0:1, 0:1] - energies[right, 0:1, 0:1]
                    mine_amps[at, low:high, :] = (numer / denom).astype(jnp.bfloat16)
                if part:
                    hand_over(at, part - 1)
            elif kind == "mine":
                apply(mine_amps[at], right, far, far not in started)
                started[far] = True
                hand_over(at, 3)
            elif kind == "other":
                size = -(-rows // (4 * LANES)) * LANES
                for piece in range(4):
                    low, high = min(piece * size, rows), min(piece * size + size, rows)
                    if high > low:
                        arrived(other_amps.at[at, pl.ds(low, high - low)], arecv_sem.at[at, piece])
                apply(other_amps[at], plane_at(k) * nx + (x + 1 - core) % nx, far, False)
            elif kind == "return":
                leave[...] = total[...].astype(jnp.bfloat16)

        for event in events:
            if event[0] == "take":
                take(*event[1:])
            elif event[0] == "send":
                send(*event[1:])
            elif event[0] == "energy":
                pass_energy(event[1])
            elif event[0] == "step":
                step(*event[1:])
            elif event[0] == "return":
                spot = pl.ds(*pieces[event[1]])
                start(remote(leave.at[spot], come.at[spot], fsend_sem.at[event[1]], frecv_sem.at[event[1]],
                             neighbour(me, "-")))
            else:
                for piece, (low, number) in enumerate(pieces):
                    spot = slice(low, low + number)
                    arrived(come.at[pl.ds(low, number)], frecv_sem.at[piece])
                    out_ref[spot, :] = out_ref[spot, :] + come[spot, :].astype(jnp.float32)
        for copy in sent:
            copy.wait_send()

    @pl.when(plane == 0)
    def _():
        run(0)

    @pl.when(plane == 1)
    def _():
        run(1)


def gathered(three_index, occ_energy, vir_energy, nz, nx, ny):
    _, rows, width = three_index.shape
    nocc, naux = nz * nx, ny * CORES
    pieces = piece_rows(rows)
    copies = max(sum(event[0] == "send" for event in program_of(plane, pieces, width)[0]) for plane in range(2))
    tasks = 5
    energy = jnp.broadcast_to(occ_energy.reshape(1, 1), (8, LANES))
    vmem = pl.BlockSpec(memory_space=pltpu.VMEM)
    dma = pltpu.SemaphoreType.DMA
    kind = three_index.dtype
    out = pl.pallas_call(
        functools.partial(gather_kernel, nz, nx, ny),
        out_shape=jax.ShapeDtypeStruct((rows, width), jnp.float32),
        in_specs=[vmem] * 4,
        out_specs=vmem,
        scratch_shapes=[
            pltpu.VMEM((nocc, rows, naux * width), kind),
            pltpu.VMEM((nocc, 8, LANES), jnp.float32),
            pltpu.VMEM((2, rows, rows), jnp.float32),
            pltpu.VMEM((tasks, rows, rows), jnp.bfloat16),
            pltpu.VMEM((tasks, rows, rows), jnp.bfloat16),
            pltpu.VMEM((rows, width), jnp.float32),
            pltpu.VMEM((rows, width), jnp.bfloat16),
            pltpu.VMEM((rows, width), jnp.bfloat16),
            dma((copies,)),
            dma((len(pieces), nocc * ny)),
            dma((len(pieces), nocc * ny)),
            dma((len(pieces), nocc * ny)),
            dma((16,)),
            dma((nocc,)),
            dma((tasks, 4)),
            dma((tasks, 4)),
            dma((len(pieces),)),
            dma((len(pieces),)),
            dma,
            dma,
        ],
        compiler_params=pltpu.CompilerParams(
            collective_id=0, has_side_effects=True, vmem_limit_bytes=48 * 1024 * 1024
        ),
    )(three_index[0], energy, vir_energy[:, None], vir_energy[None, :])
    return out[None]


def pair_amps(rows_i, eps_i, rows_j, eps_j, vir_energy):
    partial_value = lax.dot_general(
        rows_i, rows_j, (((1,), (1,)), ((), ())), preferred_element_type=jnp.float32
    )
    occ_count = eps_i.shape[0]
    vir_count = vir_energy.shape[0]
    width = occ_count * vir_count
    four = partial_value.reshape(occ_count, vir_count, occ_count, vir_count)
    numer = (2.0 * four - jnp.transpose(four, (0, 3, 2, 1))).reshape(width, width)
    denom = (
        vir_energy[None, :, None, None]
        + vir_energy[None, None, None, :]
        - eps_i[:, None, None, None]
        - eps_j[None, None, :, None]
    ).reshape(width, width)
    share = width // lax.axis_size("aux")
    mine = lax.psum_scatter(numer, "aux", scatter_dimension=0, tiled=True)
    lower = lax.axis_index("aux") * share
    denom_rows = lax.dynamic_slice_in_dim(denom, lower, share, 0)
    amps_rows = (mine / denom_rows).astype(jnp.bfloat16)
    amps = lax.all_gather(amps_rows, "aux", axis=0, tiled=True)
    return amps


def apply_other(amps, rows_i):
    return lax.dot_general(
        amps, rows_i, (((0,), (0,)), ((), ())), preferred_element_type=jnp.float32
    )


def local(three_index, occ_energy, vir_energy):
    occ_count, vir_count, aux_count = three_index.shape
    cycle_size = lax.axis_size("occ")
    my_index = lax.axis_index("occ")
    all_energy = lax.all_gather(occ_energy, "occ", axis=0, tiled=True)
    own_rows = three_index.reshape(occ_count * vir_count, aux_count)

    def energy_of(step):
        block = (my_index - step + cycle_size) % cycle_size
        return lax.dynamic_slice_in_dim(all_energy, block * occ_count, occ_count)

    amps = pair_amps(own_rows, occ_energy, own_rows, occ_energy, vir_energy)
    gamma = jnp.dot(amps, own_rows, preferred_element_type=jnp.float32)
    half = cycle_size // 2
    carried = jnp.zeros_like(gamma)

    def cycle_step(step, state):
        rows_j, carried, gamma = state
        rows_j = from_behind(rows_j, "occ", 1)
        carried = from_behind(carried, "occ", 1)
        amps = pair_amps(own_rows, occ_energy, rows_j, energy_of(step), vir_energy)
        gamma = gamma + jnp.dot(amps, rows_j, preferred_element_type=jnp.float32)
        carried = carried + apply_other(amps, own_rows)
        return (rows_j, carried, gamma)

    rows_j, carried, gamma = lax.fori_loop(1, half, cycle_step, (own_rows, carried, gamma))
    rows_j = from_behind(rows_j, "occ", 1)
    amps = pair_amps(own_rows, occ_energy, rows_j, energy_of(half), vir_energy)
    gamma = gamma + jnp.dot(amps, rows_j, preferred_element_type=jnp.float32)
    returned = from_behind(carried, "occ", 1 - half)
    gamma = gamma + returned
    return gamma.reshape(occ_count, vir_count, aux_count)


def solution(mesh):
    nocc, naux = mesh.shape["occ"], mesh.shape["aux"]

    def either(three_index, occ_energy, vir_energy):
        _, rows, width = three_index.shape
        whole = nocc * naux * three_index.size * three_index.dtype.itemsize
        pieces = len(ROUTES[0])
        fits = whole <= GATHER_LIMIT and three_index.shape[0] == 1
        fits = fits and rows % 16 == 0 and rows // 16 >= pieces and width % LANES == 0
        if fits and nocc == 8 and naux == 2 * CORES:
            return gathered(three_index, occ_energy, vir_energy, nocc // 2, 2, naux // CORES)
        return local(three_index, occ_energy, vir_energy)

    return jax.shard_map(
        either,
        mesh=mesh,
        in_specs=(P("occ", None, "aux"), P("occ"), P()),
        out_specs=P("occ", None, "aux"),
        check_vma=False,
    )
```

```python
import functools
import heapq
import itertools

import jax
import jax.numpy as jnp
from jax import lax
from jax.experimental import pallas as pl
from jax.experimental.pallas import tpu as pltpu
from jax.sharding import PartitionSpec as P

MESH = pl.DeviceIdType.MESH
CORES = 2
GATHER_LIMIT = 24 * 1024 * 1024
LANES = 128
RATE = 46250.0
HOP = 2.4
AHEAD = 2.0
SLACK = 0.0
RETURN = 3.5
ALONE = (2,)
LAST = 0
MIRROR = 2.0
MATMUL = 0.36
ELEMENT = 0.08
APPLY = 0.24
EXCHANGE = 1.4
STEP = {"x": (1, 0, 0), "y": (0, 1, 0), "+": (0, 0, 1), "-": (0, 0, -1)}
BACK = {"x": "x", "y": "y", "+": "-", "-": "+"}
ROUTES = (
    (".xyx+x+++xyy....", ".xyx+++-+++x....", ".xyx+xy++xyy....", ".xyy+-y++xy+...."),
    ("--yy.x+++xyyyy+x", "--yx.xyxx++-++xy", "yx-x.xy++xy-+x+y", "--yx.xyy+xy++xyx"),
)
URGENCY = (4, 1, -1, -2, -1, -2, -1, -1)
DEPTH = 0.5


def from_behind(array, axis, by):
    size = lax.axis_size(axis)
    return lax.ppermute(array, axis, [(i, (i + by) % size) for i in range(size)])


def moved(chip, link):
    dx, dy, dz = STEP[link]
    return ((chip[0] + dx) % 2, (chip[1] + dy) % 2, chip[2] + dz)


def piece_rows(rows):
    number = len(ROUTES[0])
    tiles = rows // 16
    lows = [16 * (tiles * at // number) for at in range(number)] + [rows]
    return [(lows[at], lows[at + 1] - lows[at]) for at in range(number)]


def routes():
    out = []
    for a, b, mirrored in itertools.product(range(2), repeat=3):
        for plane in range(2):
            for piece, text in enumerate(ROUTES[plane]):
                tree = {}
                for z, y, x in itertools.product(range(4), range(2), range(2)):
                    link = text[x + 2 * y + 4 * z]
                    if link == ".":
                        continue
                    px, py, pz = moved((x, y, z), BACK[link])
                    parent = (px ^ a, py ^ b, 3 - pz if mirrored else pz)
                    tree.setdefault(parent, []).append(BACK[link] if mirrored and link in "+-" else link)
                out.append(((a, b, 3 - plane if mirrored else plane), piece, tree))
    return out


def depth_of(tree, chip, known):
    if chip not in known:
        known[chip] = 1 + max([depth_of(tree, moved(chip, link), known) for link in tree.get(chip, ())] or [-1])
    return known[chip]


def timeline(pieces, width):
    items = routes()
    known = [{} for _ in items]
    waiting, busy, arrivals, order, heap = {}, set(), {}, {}, []
    plain = len(items)
    missing = {(x, y, z): 6 * len(pieces) for x, y, z in itertools.product(range(2), range(2), (1, 2))}
    count = itertools.count()
    for at, (source, _, _) in enumerate(items):
        heapq.heappush(heap, (0.0, next(count), True, at, source))

    def start(lane, now):
        if lane in busy or not waiting.get(lane):
            return
        _, _, at, target = heapq.heappop(waiting[lane])
        busy.add(lane)
        taken = pieces[items[at][1]][1] * width * 2 / RATE
        order.setdefault(lane, []).append((now, at))
        heapq.heappush(heap, (now + taken, next(count), False, lane, None))
        heapq.heappush(heap, (now + taken + HOP, next(count), True, at, target))

    while heap:
        now, _, arrived, at, chip = heapq.heappop(heap)
        if not arrived:
            busy.discard(at)
            start(at, now)
            continue
        source, _, tree = items[at]
        arrivals[at, chip] = now
        if at < plain and chip in missing:
            far, near = (3, 0) if chip[2] == 1 else (0, 3)
            if source[2] == far or source[::2] == (chip[0], near):
                missing[chip] -= 1
                ended = missing[chip] == 0
            else:
                ended = False
            if ended:
                for piece in range(len(pieces)):
                    items.append((chip, piece, {chip: ["-" if chip[2] == 1 else "+"]}))
                    known.append({})
                    heapq.heappush(heap, (now + RETURN, next(count), True, len(items) - 1, chip))
        for link in tree.get(chip, ()):
            target = moved(chip, link)
            plane, goal = source[2], target[2]
            if goal >= 2:
                plane, goal = 3 - plane, 3 - goal
            rank = -DEPTH * depth_of(tree, target, known[at]) - URGENCY[2 * plane + goal] if at < plain else LAST
            heapq.heappush(waiting.setdefault((chip, link), []), (rank, next(count), at, target))
            start((chip, link), now)
    return items, arrivals, order, plain


def compute_steps(ready, inner):
    own = 1 if inner else 0
    tasks, jobs = [], []
    work = [("open", 0, 0.0)] + [("matmul", part, MATMUL) for part in range(2)]
    work += [("element", part, ELEMENT) for part in range(4)] + [("mine", 0, APPLY)]

    def add(when, rank, plane, far, dx, extra=()):
        jobs.append((when, rank, len(tasks), work + list(extra)))
        tasks.append((plane, far, dx))

    for plane in sorted({key[0] for key in ready}):
        if inner and plane == 3:
            order = sorted((max(ready[plane, dx], ready[0, 0]), dx) for dx in range(2))
            add(*order[0][:1], 0, plane, True, order[0][1])
            add(*order[1][:1], 0, plane, True, order[1][1], [("return", 0, 0.1)])
        if plane in ALONE:
            for dx in range(2):
                add(max(ready[plane, dx], ready[own, 0]), 2, plane, False, dx)
        else:
            add(max(ready[plane, 0], ready[plane, 1], ready[own, 0]), 2, plane, False, None)
    steps, clock = [], 0.0
    while jobs:
        clock = max(clock, min(job[0] for job in jobs))
        job = min((job for job in jobs if job[0] <= clock), key=lambda job: (job[1], job[0], job[2]))
        kind, part, cost = job[3].pop(0)
        steps.append((clock, kind, job[2], part))
        clock += cost
        if not job[3]:
            jobs.remove(job)
        if kind == "mine" and tasks[job[2]][2] is None:
            jobs.append((clock + EXCHANGE, 1, job[2], [("other", 0, APPLY)]))
    return tasks, steps, clock


def program_of(plane, pieces, width):
    items, arrivals, order, plain = timeline(pieces, width)
    chip = (0, 0, plane)
    events = []
    ready = {}
    for at, (source, piece, _) in enumerate(items[:plain]):
        if (at, chip) in arrivals:
            key = (source[2], source[0])
            ready[key] = max(ready.get(key, 0.0), arrivals[at, chip] + MIRROR)
    tasks, steps, end = compute_steps(ready, plane == 1)
    back = max([when for when, kind, _, _ in steps if kind == "return"] or [0.0])
    first = {}
    for link in STEP:
        last = 0.0
        for when, at in order.get((chip, link), ()):
            last = max(last, arrivals[at, chip], when - AHEAD)
            if at < plain:
                first[at] = min(first.get(at, 1e9), last)
                events.append((last, 2, ("send", items[at][0], items[at][1], link)))
            else:
                events.append((max(last, back + 0.01), 4, ("return", items[at][1])))
    for at, (source, piece, _) in enumerate(items[:plain]):
        if (at, chip) in arrivals:
            when = min(arrivals[at, chip] + SLACK, first.get(at, 1e9))
            events.append((when, 1, ("take", source, piece)))
    events += [(when, 3, ("step", *step)) for when, *step in steps]
    for away in range(4 if plane == 1 else 3):
        if away != plane:
            events.append((5.0 * abs(away - plane), 0, ("energy", away)))
    if plane == 0:
        events.append((end + 100.0, 4, ("far",)))
    events.sort(key=lambda event: event[:2])
    return [event[2] for event in events], tasks


def gather_kernel(nz, nx, ny, hbm_ref, occ_ref, row_ref, out_ref, b_ref, e_ref, col_ref, blocks, energies, value, mine_amps, other_amps,
                  total, leave, come, send_sem, recv_sem, msend_sem, mrecv_sem, esend_sem, erecv_sem,
                  asend_sem, arecv_sem, fsend_sem, frecv_sem, keep_sem, load_sem, unused_sem):
    rows, width = b_ref.shape
    occ, aux = lax.axis_index("occ"), lax.axis_index("aux")
    z, x = occ // nx, occ % nx
    y, core = aux // CORES, aux % CORES
    upper = z // 2
    plane = z + upper * (nz - 1 - 2 * z)
    pieces = piece_rows(rows)

    def plane_at(k):
        return k + upper * (nz - 1 - 2 * k)

    def block_at(dx, k):
        return plane_at(k) * nx + (x + dx) % nx

    def device(dx, dy, k, dc=0):
        return block_at(dx, k), ((y + dy) % ny) * CORES + (core + dc) % CORES

    def neighbour(me, link):
        dx, dy, dz = STEP[link]
        return device(dx, dy, me + dz)

    def columns(shard_aux):
        return pl.ds(pl.multiple_of(shard_aux * width, width), width)

    keep = pltpu.make_async_copy(b_ref, blocks.at[occ, :, columns(aux)], keep_sem)
    load = pltpu.make_async_copy(hbm_ref, b_ref, load_sem)
    load.start()
    partner = (occ, y * CORES + (core + 1) % CORES)
    barrier = pltpu.get_barrier_semaphore()
    step_up = 1 - 2 * upper
    near = [
        partner,
        (z * nx + (x + 1) % nx, aux),
        (occ, ((y + 1) % ny) * CORES + core),
        ((z + step_up) * nx + x, aux),
    ]
    for target in near:
        pl.semaphore_signal(barrier, inc=1, device_id=target, device_id_type=MESH)

    @pl.when(plane == 1)
    def _():
        pl.semaphore_signal(barrier, inc=1, device_id=((z - step_up) * nx + x, aux), device_id_type=MESH)

    e_ref[...] = jnp.full(e_ref.shape, occ_ref[0], jnp.float32)
    col_ref[...] = jnp.broadcast_to(row_ref[...], (8, rows)).T[:, 0:1]
    load.wait()
    keep.start()
    pl.semaphore_wait(barrier, len(near) + plane)

    def run(me):
        events, tasks = program_of(me, pieces, width)
        sent = []
        taken = set()
        started = {}

        def place(source, piece, dc=0):
            block, shard_aux = device(source[0], source[1], source[2], dc)
            low, number = pieces[piece]
            return blocks.at[block, pl.ds(low, number), columns(shard_aux)]

        def chip_index(source):
            block, shard_aux = device(*source)
            return block * ny + shard_aux // CORES

        def origin(source, piece):
            low, number = pieces[piece]
            return b_ref.at[pl.ds(low, number)] if source == (0, 0, me) else place(source, piece)

        def remote(src, dst, send, recv, target):
            return pltpu.make_async_remote_copy(
                src_ref=src, dst_ref=dst, send_sem=send, recv_sem=recv, device_id=target, device_id_type=MESH
            )

        def start(copy):
            copy.start()
            sent.append(copy)

        def arrived(spot, sem):
            remote(spot, spot, unused_sem, sem, (occ, aux)).wait_recv()

        for target in ["x", "+"] + (["-"] if me == 1 else []):
            start(remote(e_ref, energies.at[occ], esend_sem.at[len(sent)], erecv_sem.at[occ], neighbour(me, target)))
        number_sent = [0]

        def send(source, piece, link):
            copy = remote(
                origin(source, piece), place(source, piece), send_sem.at[number_sent[0]],
                recv_sem.at[piece, chip_index(source)], neighbour(me, link),
            )
            number_sent[0] += 1
            start(copy)

        def take(source, piece):
            if source != (0, 0, me):
                arrived(place(source, piece), recv_sem.at[piece, chip_index(source)])
            start(remote(
                origin(source, piece), place(source, piece), msend_sem.at[piece, chip_index(source)],
                mrecv_sem.at[piece, chip_index(source)], partner,
            ))

        def pass_energy(away):
            if away in passed:
                return
            passed.add(away)
            block = block_at(0, away)
            arrived(energies.at[block], erecv_sem.at[block])
            onward = ["x"] + ({0: ["+"], 2: ["-"]}.get(away, []) if me == 1 else [])
            for link in onward:
                start(remote(energies.at[block], energies.at[block], esend_sem.at[count_energy[0]],
                             erecv_sem.at[block], neighbour(me, link)))
                count_energy[0] += 1

        count_energy = [len(sent)]
        passed = {me}
        energies[occ] = e_ref[...]

        def open_block(dx, k):
            if (dx, k) in taken:
                return
            taken.add((dx, k))
            if dx == 0:
                pass_energy(k)
            else:
                block = block_at(1, k)
                arrived(energies.at[block], erecv_sem.at[block])
            if (dx, k) == (0, me):
                keep.wait()
            for source in itertools.product([dx], range(2), [k]):
                for piece in range(len(pieces)):
                    arrived(place(source, piece, 1), mrecv_sem.at[piece, chip_index(source)])

        def hand_over(at, part):
            size = -(-rows // (4 * LANES)) * LANES
            low, high = min(part * size, rows), min(part * size + size, rows)
            if high > low:
                spot = pl.ds(low, high - low)
                start(remote(mine_amps.at[at, spot], other_amps.at[at, spot], asend_sem.at[at, part],
                             arecv_sem.at[at, part], partner))

        def apply(amps, block, far, fresh):
            term = jnp.dot(amps, blocks[block, :, columns(aux)], preferred_element_type=jnp.float32)
            goal = total if far else out_ref
            goal[...] = term if fresh else goal[...] + term

        def step(kind, at, part):
            k, far, dx = tasks[at]
            left = block_at(0, 0) if far else occ
            right = plane_at(k) * nx + (x + (core if dx is None else dx)) % nx
            if kind == "open":
                open_block(0, 0 if far else me)
                for which in range(2) if dx is None else [dx]:
                    open_block(which, k)
            elif kind == "matmul":
                cut = rows // 2 // LANES * LANES + LANES if rows > LANES else rows
                low, high = ((0, min(cut, rows)), (min(cut, rows), rows))[part]
                if high > low:
                    value[int(far), :, low:high] = lax.dot_general(
                        blocks[left], blocks[right, low:high, :], (((1,), (1,)), ((), ())),
                        preferred_element_type=jnp.float32,
                    )
            elif kind == "element":
                size = -(-rows // (4 * LANES)) * LANES
                low, high = min(part * size, rows), min(part * size + size, rows)
                if high > low:
                    numer = 2.0 * value[int(far), low:high, :] - value[int(far), :, low:high].T
                    denom = col_ref[low:high, :] + row_ref[...] - energies[left, 0:1, 0:1] - energies[right, 0:1, 0:1]
                    mine_amps[at, low:high, :] = (numer / denom).astype(jnp.bfloat16)
                if part and dx is None:
                    hand_over(at, part - 1)
            elif kind == "mine":
                apply(mine_amps[at], right, far, far not in started)
                started[far] = True
                if dx is None:
                    hand_over(at, 3)
            elif kind == "other":
                size = -(-rows // (4 * LANES)) * LANES
                for piece in range(4):
                    low, high = min(piece * size, rows), min(piece * size + size, rows)
                    if high > low:
                        arrived(other_amps.at[at, pl.ds(low, high - low)], arecv_sem.at[at, piece])
                apply(other_amps[at], plane_at(k) * nx + (x + 1 - core) % nx, far, False)
            elif kind == "return":
                leave[...] = total[...].astype(jnp.bfloat16)

        for event in events:
            if event[0] == "take":
                take(*event[1:])
            elif event[0] == "send":
                send(*event[1:])
            elif event[0] == "energy":
                pass_energy(event[1])
            elif event[0] == "step":
                step(*event[1:])
            elif event[0] == "return":
                spot = pl.ds(*pieces[event[1]])
                start(remote(leave.at[spot], come.at[spot], fsend_sem.at[event[1]], frecv_sem.at[event[1]],
                             neighbour(me, "-")))
            else:
                for piece, (low, number) in enumerate(pieces):
                    spot = slice(low, low + number)
                    arrived(come.at[pl.ds(low, number)], frecv_sem.at[piece])
                    out_ref[spot, :] = out_ref[spot, :] + come[spot, :].astype(jnp.float32)
        for copy in sent:
            copy.wait_send()

    @pl.when(plane == 0)
    def _():
        run(0)

    @pl.when(plane == 1)
    def _():
        run(1)


def gathered(three_index, occ_energy, vir_energy, nz, nx, ny):
    _, rows, width = three_index.shape
    nocc, naux = nz * nx, ny * CORES
    pieces = piece_rows(rows)
    copies = max(sum(event[0] == "send" for event in program_of(plane, pieces, width)[0]) for plane in range(2))
    tasks = max(len(program_of(plane, pieces, width)[1]) for plane in range(2))
    vmem = pl.BlockSpec(memory_space=pltpu.VMEM)
    dma = pltpu.SemaphoreType.DMA
    kind = three_index.dtype
    out = pl.pallas_call(
        functools.partial(gather_kernel, nz, nx, ny),
        out_shape=jax.ShapeDtypeStruct((rows, width), jnp.float32),
        in_specs=[pl.BlockSpec(memory_space=pltpu.HBM), pl.BlockSpec(memory_space=pltpu.SMEM), vmem],
        out_specs=vmem,
        scratch_shapes=[
            pltpu.VMEM((rows, width), kind),
            pltpu.VMEM((8, LANES), jnp.float32),
            pltpu.VMEM((rows, 1), jnp.float32),
            pltpu.VMEM((nocc, rows, naux * width), kind),
            pltpu.VMEM((nocc, 8, LANES), jnp.float32),
            pltpu.VMEM((2, rows, rows), jnp.float32),
            pltpu.VMEM((tasks, rows, rows), jnp.bfloat16),
            pltpu.VMEM((tasks, rows, rows), jnp.bfloat16),
            pltpu.VMEM((rows, width), jnp.float32),
            pltpu.VMEM((rows, width), jnp.bfloat16),
            pltpu.VMEM((rows, width), jnp.bfloat16),
            dma((copies,)),
            dma((len(pieces), nocc * ny)),
            dma((len(pieces), nocc * ny)),
            dma((len(pieces), nocc * ny)),
            dma((16,)),
            dma((nocc,)),
            dma((tasks, 4)),
            dma((tasks, 4)),
            dma((len(pieces),)),
            dma((len(pieces),)),
            dma,
            dma,
            dma,
        ],
        compiler_params=pltpu.CompilerParams(
            collective_id=0, has_side_effects=True, vmem_limit_bytes=48 * 1024 * 1024
        ),
    )(three_index[0], occ_energy, vir_energy[None, :])
    return out[None]


def pair_amps(rows_i, eps_i, rows_j, eps_j, vir_energy):
    partial_value = lax.dot_general(
        rows_i, rows_j, (((1,), (1,)), ((), ())), preferred_element_type=jnp.float32
    )
    occ_count = eps_i.shape[0]
    vir_count = vir_energy.shape[0]
    width = occ_count * vir_count
    four = partial_value.reshape(occ_count, vir_count, occ_count, vir_count)
    numer = (2.0 * four - jnp.transpose(four, (0, 3, 2, 1))).reshape(width, width)
    denom = (
        vir_energy[None, :, None, None]
        + vir_energy[None, None, None, :]
        - eps_i[:, None, None, None]
        - eps_j[None, None, :, None]
    ).reshape(width, width)
    share = width // lax.axis_size("aux")
    mine = lax.psum_scatter(numer, "aux", scatter_dimension=0, tiled=True)
    lower = lax.axis_index("aux") * share
    denom_rows = lax.dynamic_slice_in_dim(denom, lower, share, 0)
    amps_rows = (mine / denom_rows).astype(jnp.bfloat16)
    amps = lax.all_gather(amps_rows, "aux", axis=0, tiled=True)
    return amps


def apply_other(amps, rows_i):
    return lax.dot_general(
        amps, rows_i, (((0,), (0,)), ((), ())), preferred_element_type=jnp.float32
    )


def local(three_index, occ_energy, vir_energy):
    occ_count, vir_count, aux_count = three_index.shape
    cycle_size = lax.axis_size("occ")
    my_index = lax.axis_index("occ")
    all_energy = lax.all_gather(occ_energy, "occ", axis=0, tiled=True)
    own_rows = three_index.reshape(occ_count * vir_count, aux_count)

    def energy_of(step):
        block = (my_index - step + cycle_size) % cycle_size
        return lax.dynamic_slice_in_dim(all_energy, block * occ_count, occ_count)

    amps = pair_amps(own_rows, occ_energy, own_rows, occ_energy, vir_energy)
    gamma = jnp.dot(amps, own_rows, preferred_element_type=jnp.float32)
    half = cycle_size // 2
    carried = jnp.zeros_like(gamma)

    def cycle_step(step, state):
        rows_j, carried, gamma = state
        rows_j = from_behind(rows_j, "occ", 1)
        carried = from_behind(carried, "occ", 1)
        amps = pair_amps(own_rows, occ_energy, rows_j, energy_of(step), vir_energy)
        gamma = gamma + jnp.dot(amps, rows_j, preferred_element_type=jnp.float32)
        carried = carried + apply_other(amps, own_rows)
        return (rows_j, carried, gamma)

    rows_j, carried, gamma = lax.fori_loop(1, half, cycle_step, (own_rows, carried, gamma))
    rows_j = from_behind(rows_j, "occ", 1)
    amps = pair_amps(own_rows, occ_energy, rows_j, energy_of(half), vir_energy)
    gamma = gamma + jnp.dot(amps, rows_j, preferred_element_type=jnp.float32)
    returned = from_behind(carried, "occ", 1 - half)
    gamma = gamma + returned
    return gamma.reshape(occ_count, vir_count, aux_count)


def solution(mesh):
    nocc, naux = mesh.shape["occ"], mesh.shape["aux"]

    def either(three_index, occ_energy, vir_energy):
        _, rows, width = three_index.shape
        whole = nocc * naux * three_index.size * three_index.dtype.itemsize
        pieces = len(ROUTES[0])
        fits = whole <= GATHER_LIMIT and three_index.shape[0] == 1
        fits = fits and rows % 16 == 0 and rows // 16 >= pieces and width % LANES == 0
        if fits and nocc == 8 and naux == 2 * CORES:
            return gathered(three_index, occ_energy, vir_energy, nocc // 2, 2, naux // CORES)
        return local(three_index, occ_energy, vir_energy)

    return jax.shard_map(
        either,
        mesh=mesh,
        in_specs=(P("occ", None, "aux"), P("occ"), P()),
        out_specs=P("occ", None, "aux"),
        check_vma=False,
    )
```

```python
import functools
import heapq
import itertools

import jax
import jax.numpy as jnp
from jax import lax
from jax.experimental import pallas as pl
from jax.experimental.pallas import tpu as pltpu
from jax.sharding import PartitionSpec as P

MESH = pl.DeviceIdType.MESH
CORES = 2
GATHER_LIMIT = 24 * 1024 * 1024
LANES = 128
RATE = 46250.0
HOP = 2.6
AHEAD = 2.0
SLACK = 0.0
RETURN = 3.5
ALONE = (2,)
LAST = 0
MIRROR = 2.0
MATMUL = 0.36
ELEMENT = 0.08
APPLY = 0.24
EXCHANGE = 1.4
STEP = {"x": (1, 0, 0), "y": (0, 1, 0), "+": (0, 0, 1), "-": (0, 0, -1)}
BACK = {"x": "x", "y": "y", "+": "-", "-": "+"}
ROUTES = (
    (".xyx+x+++xyy....", ".xyx+++-+++x....", ".xyx+xy++xyy....", ".xyy+-y++xy+...."),
    ("--yy.x+++xyyyy+x", "--yx.xyxx++-++xy", "yx-x.xy++xy-+x+y", "--yx.xyy+xy++xyx"),
)
URGENCY = (4, 1, -1, -2, -1, -2, -1, -1)
DEPTH = 0.5


def from_behind(array, axis, by):
    size = lax.axis_size(axis)
    return lax.ppermute(array, axis, [(i, (i + by) % size) for i in range(size)])


def moved(chip, link):
    dx, dy, dz = STEP[link]
    return ((chip[0] + dx) % 2, (chip[1] + dy) % 2, chip[2] + dz)


def piece_rows(rows):
    number = len(ROUTES[0])
    tiles = rows // 16
    lows = [16 * (tiles * at // number) for at in range(number)] + [rows]
    return [(lows[at], lows[at + 1] - lows[at]) for at in range(number)]


def routes():
    out = []
    for a, b, mirrored in itertools.product(range(2), repeat=3):
        for plane in range(2):
            for piece, text in enumerate(ROUTES[plane]):
                tree = {}
                for z, y, x in itertools.product(range(4), range(2), range(2)):
                    link = text[x + 2 * y + 4 * z]
                    if link == ".":
                        continue
                    px, py, pz = moved((x, y, z), BACK[link])
                    parent = (px ^ a, py ^ b, 3 - pz if mirrored else pz)
                    tree.setdefault(parent, []).append(BACK[link] if mirrored and link in "+-" else link)
                out.append(((a, b, 3 - plane if mirrored else plane), piece, tree))
    return out


def depth_of(tree, chip, known):
    if chip not in known:
        known[chip] = 1 + max([depth_of(tree, moved(chip, link), known) for link in tree.get(chip, ())] or [-1])
    return known[chip]


def timeline(pieces, width):
    items = routes()
    known = [{} for _ in items]
    waiting, busy, arrivals, order, heap = {}, set(), {}, {}, []
    plain = len(items)
    missing = {(x, y, z): 6 * len(pieces) for x, y, z in itertools.product(range(2), range(2), (1, 2))}
    count = itertools.count()
    for at, (source, _, _) in enumerate(items):
        heapq.heappush(heap, (0.0, next(count), True, at, source))

    def start(lane, now):
        if lane in busy or not waiting.get(lane):
            return
        _, _, at, target = heapq.heappop(waiting[lane])
        busy.add(lane)
        taken = pieces[items[at][1]][1] * width * 2 / RATE
        order.setdefault(lane, []).append((now, at))
        heapq.heappush(heap, (now + taken, next(count), False, lane, None))
        heapq.heappush(heap, (now + taken + HOP, next(count), True, at, target))

    while heap:
        now, _, arrived, at, chip = heapq.heappop(heap)
        if not arrived:
            busy.discard(at)
            start(at, now)
            continue
        source, _, tree = items[at]
        arrivals[at, chip] = now
        if at < plain and chip in missing:
            far, near = (3, 0) if chip[2] == 1 else (0, 3)
            if source[2] == far or source[::2] == (chip[0], near):
                missing[chip] -= 1
                ended = missing[chip] == 0
            else:
                ended = False
            if ended:
                for piece in range(len(pieces)):
                    items.append((chip, piece, {chip: ["-" if chip[2] == 1 else "+"]}))
                    known.append({})
                    heapq.heappush(heap, (now + RETURN, next(count), True, len(items) - 1, chip))
        for link in tree.get(chip, ()):
            target = moved(chip, link)
            plane, goal = source[2], target[2]
            if goal >= 2:
                plane, goal = 3 - plane, 3 - goal
            rank = -DEPTH * depth_of(tree, target, known[at]) - URGENCY[2 * plane + goal] if at < plain else LAST
            heapq.heappush(waiting.setdefault((chip, link), []), (rank, next(count), at, target))
            start((chip, link), now)
    return items, arrivals, order, plain


def compute_steps(ready, inner):
    own = 1 if inner else 0
    tasks, jobs = [], []
    work = [("open", 0, 0.0)] + [("matmul", part, MATMUL) for part in range(2)]
    work += [("element", part, ELEMENT) for part in range(4)] + [("mine", 0, APPLY)]

    def add(when, rank, plane, far, dx, extra=()):
        jobs.append((when, rank, len(tasks), work + list(extra)))
        tasks.append((plane, far, dx))

    for plane in sorted({key[0] for key in ready}):
        if inner and plane == 3:
            order = sorted((max(ready[plane, dx], ready[0, 0]), dx) for dx in range(2))
            add(*order[0][:1], 0, plane, True, order[0][1])
            add(*order[1][:1], 0, plane, True, order[1][1], [("return", 0, 0.1)])
        if plane in ALONE:
            for dx in range(2):
                add(max(ready[plane, dx], ready[own, 0]), 2, plane, False, dx)
        else:
            add(max(ready[plane, 0], ready[plane, 1], ready[own, 0]), 2, plane, False, None)
    steps, clock = [], 0.0
    while jobs:
        clock = max(clock, min(job[0] for job in jobs))
        job = min((job for job in jobs if job[0] <= clock), key=lambda job: (job[1], job[0], job[2]))
        kind, part, cost = job[3].pop(0)
        steps.append((clock, kind, job[2], part))
        clock += cost
        if not job[3]:
            jobs.remove(job)
        if kind == "mine" and tasks[job[2]][2] is None:
            jobs.append((clock + EXCHANGE, 1, job[2], [("other", 0, APPLY)]))
    return tasks, steps, clock


def program_of(plane, pieces, width):
    items, arrivals, order, plain = timeline(pieces, width)
    chip = (0, 0, plane)
    events = []
    ready = {}
    for at, (source, piece, _) in enumerate(items[:plain]):
        if (at, chip) in arrivals:
            key = (source[2], source[0])
            ready[key] = max(ready.get(key, 0.0), arrivals[at, chip] + MIRROR)
    tasks, steps, end = compute_steps(ready, plane == 1)
    back = max([when for when, kind, _, _ in steps if kind == "return"] or [0.0])
    first = {}
    for link in STEP:
        last = 0.0
        for when, at in order.get((chip, link), ()):
            last = max(last, arrivals[at, chip], when - AHEAD)
            if at < plain:
                first[at] = min(first.get(at, 1e9), last)
                events.append((last, 2, ("send", items[at][0], items[at][1], link)))
            else:
                events.append((max(last, back + 0.01), 4, ("return", items[at][1])))
    for at, (source, piece, _) in enumerate(items[:plain]):
        if (at, chip) in arrivals:
            when = 1.0 if source == chip else min(arrivals[at, chip] + SLACK, first.get(at, 1e9))
            events.append((when, 1, ("take", source, piece)))
    events += [(when, 3, ("step", *step)) for when, *step in steps]
    for away in range(4 if plane == 1 else 3):
        if away != plane:
            events.append((5.0 * abs(away - plane), 0, ("energy", away)))
    if plane == 0:
        events.append((end + 100.0, 4, ("far",)))
    events.sort(key=lambda event: event[:2])
    return [event[2] for event in events], tasks


def gather_kernel(nz, nx, ny, hbm_ref, occ_ref, row_ref, out_ref, b_ref, e_ref, col_ref, blocks, energies, value, mine_amps, other_amps,
                  total, leave, come, send_sem, recv_sem, msend_sem, mrecv_sem, esend_sem, erecv_sem,
                  asend_sem, arecv_sem, fsend_sem, frecv_sem, keep_sem, load_sem, unused_sem):
    rows, width = b_ref.shape
    occ, aux = lax.axis_index("occ"), lax.axis_index("aux")
    z, x = occ // nx, occ % nx
    y, core = aux // CORES, aux % CORES
    upper = z // 2
    plane = z + upper * (nz - 1 - 2 * z)
    pieces = piece_rows(rows)

    def plane_at(k):
        return k + upper * (nz - 1 - 2 * k)

    def block_at(dx, k):
        return plane_at(k) * nx + (x + dx) % nx

    def device(dx, dy, k, dc=0):
        return block_at(dx, k), ((y + dy) % ny) * CORES + (core + dc) % CORES

    def neighbour(me, link):
        dx, dy, dz = STEP[link]
        return device(dx, dy, me + dz)

    def columns(shard_aux):
        return pl.ds(pl.multiple_of(shard_aux * width, width), width)

    keep = pltpu.make_async_copy(b_ref, blocks.at[occ, :, columns(aux)], keep_sem)
    load = pltpu.make_async_copy(hbm_ref, b_ref, load_sem)
    load.start()
    partner = (occ, y * CORES + (core + 1) % CORES)
    barrier = pltpu.get_barrier_semaphore()
    step_up = 1 - 2 * upper
    near = [
        partner,
        (z * nx + (x + 1) % nx, aux),
        (occ, ((y + 1) % ny) * CORES + core),
        ((z + step_up) * nx + x, aux),
    ]
    for target in near:
        pl.semaphore_signal(barrier, inc=1, device_id=target, device_id_type=MESH)

    @pl.when(plane == 1)
    def _():
        pl.semaphore_signal(barrier, inc=1, device_id=((z - step_up) * nx + x, aux), device_id_type=MESH)

    e_ref[...] = jnp.full(e_ref.shape, occ_ref[0], jnp.float32)
    col_ref[...] = jnp.broadcast_to(row_ref[...], (8, rows)).T[:, 0:1]
    load.wait()
    keep.start()
    pl.semaphore_wait(barrier, len(near) + plane)

    def run(me):
        events, tasks = program_of(me, pieces, width)
        sent = []
        taken = set()
        started = {}

        def place(source, piece, dc=0):
            block, shard_aux = device(source[0], source[1], source[2], dc)
            low, number = pieces[piece]
            return blocks.at[block, pl.ds(low, number), columns(shard_aux)]

        def chip_index(source):
            block, shard_aux = device(*source)
            return block * ny + shard_aux // CORES

        def origin(source, piece):
            low, number = pieces[piece]
            return b_ref.at[pl.ds(low, number)] if source == (0, 0, me) else place(source, piece)

        def remote(src, dst, send, recv, target):
            return pltpu.make_async_remote_copy(
                src_ref=src, dst_ref=dst, send_sem=send, recv_sem=recv, device_id=target, device_id_type=MESH
            )

        def start(copy):
            copy.start()
            sent.append(copy)

        def arrived(spot, sem):
            remote(spot, spot, unused_sem, sem, (occ, aux)).wait_recv()

        for target in ["x", "+"] + (["-"] if me == 1 else []):
            start(remote(e_ref, energies.at[occ], esend_sem.at[len(sent)], erecv_sem.at[occ], neighbour(me, target)))
        number_sent = [0]

        def send(source, piece, link):
            copy = remote(
                origin(source, piece), place(source, piece), send_sem.at[number_sent[0]],
                recv_sem.at[piece, chip_index(source)], neighbour(me, link),
            )
            number_sent[0] += 1
            start(copy)

        def take(source, piece):
            if source != (0, 0, me):
                arrived(place(source, piece), recv_sem.at[piece, chip_index(source)])
            start(remote(
                origin(source, piece), place(source, piece), msend_sem.at[piece, chip_index(source)],
                mrecv_sem.at[piece, chip_index(source)], partner,
            ))

        def pass_energy(away):
            if away in passed:
                return
            passed.add(away)
            block = block_at(0, away)
            arrived(energies.at[block], erecv_sem.at[block])
            onward = ["x"] + ({0: ["+"], 2: ["-"]}.get(away, []) if me == 1 else [])
            for link in onward:
                start(remote(energies.at[block], energies.at[block], esend_sem.at[count_energy[0]],
                             erecv_sem.at[block], neighbour(me, link)))
                count_energy[0] += 1

        count_energy = [len(sent)]
        passed = {me}
        energies[occ] = e_ref[...]

        def open_block(dx, k):
            if (dx, k) in taken:
                return
            taken.add((dx, k))
            if dx == 0:
                pass_energy(k)
            else:
                block = block_at(1, k)
                arrived(energies.at[block], erecv_sem.at[block])
            if (dx, k) == (0, me):
                keep.wait()
            for source in itertools.product([dx], range(2), [k]):
                for piece in range(len(pieces)):
                    arrived(place(source, piece, 1), mrecv_sem.at[piece, chip_index(source)])

        def hand_over(at, part):
            size = -(-rows // (4 * LANES)) * LANES
            low, high = min(part * size, rows), min(part * size + size, rows)
            if high > low:
                spot = pl.ds(low, high - low)
                start(remote(mine_amps.at[at, spot], other_amps.at[at, spot], asend_sem.at[at, part],
                             arecv_sem.at[at, part], partner))

        def apply(amps, block, far, fresh):
            term = jnp.dot(amps, blocks[block, :, columns(aux)], preferred_element_type=jnp.float32)
            goal = total if far else out_ref
            goal[...] = term if fresh else goal[...] + term

        def step(kind, at, part):
            k, far, dx = tasks[at]
            left = block_at(0, 0) if far else occ
            right = plane_at(k) * nx + (x + (core if dx is None else dx)) % nx
            if kind == "open":
                open_block(0, 0 if far else me)
                for which in range(2) if dx is None else [dx]:
                    open_block(which, k)
            elif kind == "matmul":
                cut = rows // 2 // LANES * LANES + LANES if rows > LANES else rows
                low, high = ((0, min(cut, rows)), (min(cut, rows), rows))[part]
                if high > low:
                    value[int(far), :, low:high] = lax.dot_general(
                        blocks[left], blocks[right, low:high, :], (((1,), (1,)), ((), ())),
                        preferred_element_type=jnp.float32,
                    )
            elif kind == "element":
                size = -(-rows // (4 * LANES)) * LANES
                low, high = min(part * size, rows), min(part * size + size, rows)
                if high > low:
                    numer = 2.0 * value[int(far), low:high, :] - value[int(far), :, low:high].T
                    denom = col_ref[low:high, :] + row_ref[...] - energies[left, 0:1, 0:1] - energies[right, 0:1, 0:1]
                    mine_amps[at, low:high, :] = (numer / denom).astype(jnp.bfloat16)
                if part and dx is None:
                    hand_over(at, part - 1)
            elif kind == "mine":
                apply(mine_amps[at], right, far, far not in started)
                started[far] = True
                if dx is None:
                    hand_over(at, 3)
            elif kind == "other":
                size = -(-rows // (4 * LANES)) * LANES
                for piece in range(4):
                    low, high = min(piece * size, rows), min(piece * size + size, rows)
                    if high > low:
                        arrived(other_amps.at[at, pl.ds(low, high - low)], arecv_sem.at[at, piece])
                apply(other_amps[at], plane_at(k) * nx + (x + 1 - core) % nx, far, False)
            elif kind == "return":
                leave[...] = total[...].astype(jnp.bfloat16)

        for event in events:
            if event[0] == "take":
                take(*event[1:])
            elif event[0] == "send":
                send(*event[1:])
            elif event[0] == "energy":
                pass_energy(event[1])
            elif event[0] == "step":
                step(*event[1:])
            elif event[0] == "return":
                spot = pl.ds(*pieces[event[1]])
                start(remote(leave.at[spot], come.at[spot], fsend_sem.at[event[1]], frecv_sem.at[event[1]],
                             neighbour(me, "-")))
            else:
                for piece, (low, number) in enumerate(pieces):
                    spot = slice(low, low + number)
                    arrived(come.at[pl.ds(low, number)], frecv_sem.at[piece])
                    out_ref[spot, :] = out_ref[spot, :] + come[spot, :].astype(jnp.float32)
        for copy in sent:
            copy.wait_send()

    @pl.when(plane == 0)
    def _():
        run(0)

    @pl.when(plane == 1)
    def _():
        run(1)


def gathered(three_index, occ_energy, vir_energy, nz, nx, ny):
    _, rows, width = three_index.shape
    nocc, naux = nz * nx, ny * CORES
    pieces = piece_rows(rows)
    copies = max(sum(event[0] == "send" for event in program_of(plane, pieces, width)[0]) for plane in range(2))
    tasks = max(len(program_of(plane, pieces, width)[1]) for plane in range(2))
    vmem = pl.BlockSpec(memory_space=pltpu.VMEM)
    dma = pltpu.SemaphoreType.DMA
    kind = three_index.dtype
    out = pl.pallas_call(
        functools.partial(gather_kernel, nz, nx, ny),
        out_shape=jax.ShapeDtypeStruct((rows, width), jnp.float32),
        in_specs=[pl.BlockSpec(memory_space=pltpu.HBM), pl.BlockSpec(memory_space=pltpu.SMEM), vmem],
        out_specs=vmem,
        scratch_shapes=[
            pltpu.VMEM((rows, width), kind),
            pltpu.VMEM((8, LANES), jnp.float32),
            pltpu.VMEM((rows, 1), jnp.float32),
            pltpu.VMEM((nocc, rows, naux * width), kind),
            pltpu.VMEM((nocc, 8, LANES), jnp.float32),
            pltpu.VMEM((2, rows, rows), jnp.float32),
            pltpu.VMEM((tasks, rows, rows), jnp.bfloat16),
            pltpu.VMEM((tasks, rows, rows), jnp.bfloat16),
            pltpu.VMEM((rows, width), jnp.float32),
            pltpu.VMEM((rows, width), jnp.bfloat16),
            pltpu.VMEM((rows, width), jnp.bfloat16),
            dma((copies,)),
            dma((len(pieces), nocc * ny)),
            dma((len(pieces), nocc * ny)),
            dma((len(pieces), nocc * ny)),
            dma((16,)),
            dma((nocc,)),
            dma((tasks, 4)),
            dma((tasks, 4)),
            dma((len(pieces),)),
            dma((len(pieces),)),
            dma,
            dma,
            dma,
        ],
        compiler_params=pltpu.CompilerParams(
            collective_id=0, has_side_effects=True, vmem_limit_bytes=48 * 1024 * 1024
        ),
    )(three_index[0], occ_energy, vir_energy[None, :])
    return out[None]


def pair_amps(rows_i, eps_i, rows_j, eps_j, vir_energy):
    partial_value = lax.dot_general(
        rows_i, rows_j, (((1,), (1,)), ((), ())), preferred_element_type=jnp.float32
    )
    occ_count = eps_i.shape[0]
    vir_count = vir_energy.shape[0]
    width = occ_count * vir_count
    four = partial_value.reshape(occ_count, vir_count, occ_count, vir_count)
    numer = (2.0 * four - jnp.transpose(four, (0, 3, 2, 1))).reshape(width, width)
    denom = (
        vir_energy[None, :, None, None]
        + vir_energy[None, None, None, :]
        - eps_i[:, None, None, None]
        - eps_j[None, None, :, None]
    ).reshape(width, width)
    share = width // lax.axis_size("aux")
    mine = lax.psum_scatter(numer, "aux", scatter_dimension=0, tiled=True)
    lower = lax.axis_index("aux") * share
    denom_rows = lax.dynamic_slice_in_dim(denom, lower, share, 0)
    amps_rows = (mine / denom_rows).astype(jnp.bfloat16)
    amps = lax.all_gather(amps_rows, "aux", axis=0, tiled=True)
    return amps


def apply_other(amps, rows_i):
    return lax.dot_general(
        amps, rows_i, (((0,), (0,)), ((), ())), preferred_element_type=jnp.float32
    )


def local(three_index, occ_energy, vir_energy):
    occ_count, vir_count, aux_count = three_index.shape
    cycle_size = lax.axis_size("occ")
    my_index = lax.axis_index("occ")
    all_energy = lax.all_gather(occ_energy, "occ", axis=0, tiled=True)
    own_rows = three_index.reshape(occ_count * vir_count, aux_count)

    def energy_of(step):
        block = (my_index - step + cycle_size) % cycle_size
        return lax.dynamic_slice_in_dim(all_energy, block * occ_count, occ_count)

    amps = pair_amps(own_rows, occ_energy, own_rows, occ_energy, vir_energy)
    gamma = jnp.dot(amps, own_rows, preferred_element_type=jnp.float32)
    half = cycle_size // 2
    carried = jnp.zeros_like(gamma)

    def cycle_step(step, state):
        rows_j, carried, gamma = state
        rows_j = from_behind(rows_j, "occ", 1)
        carried = from_behind(carried, "occ", 1)
        amps = pair_amps(own_rows, occ_energy, rows_j, energy_of(step), vir_energy)
        gamma = gamma + jnp.dot(amps, rows_j, preferred_element_type=jnp.float32)
        carried = carried + apply_other(amps, own_rows)
        return (rows_j, carried, gamma)

    rows_j, carried, gamma = lax.fori_loop(1, half, cycle_step, (own_rows, carried, gamma))
    rows_j = from_behind(rows_j, "occ", 1)
    amps = pair_amps(own_rows, occ_energy, rows_j, energy_of(half), vir_energy)
    gamma = gamma + jnp.dot(amps, rows_j, preferred_element_type=jnp.float32)
    returned = from_behind(carried, "occ", 1 - half)
    gamma = gamma + returned
    return gamma.reshape(occ_count, vir_count, aux_count)


def solution(mesh):
    nocc, naux = mesh.shape["occ"], mesh.shape["aux"]

    def either(three_index, occ_energy, vir_energy):
        _, rows, width = three_index.shape
        whole = nocc * naux * three_index.size * three_index.dtype.itemsize
        pieces = len(ROUTES[0])
        fits = whole <= GATHER_LIMIT and three_index.shape[0] == 1
        fits = fits and rows % 16 == 0 and rows // 16 >= pieces and width % LANES == 0
        if fits and nocc == 8 and naux == 2 * CORES:
            return gathered(three_index, occ_energy, vir_energy, nocc // 2, 2, naux // CORES)
        return local(three_index, occ_energy, vir_energy)

    return jax.shard_map(
        either,
        mesh=mesh,
        in_specs=(P("occ", None, "aux"), P("occ"), P()),
        out_specs=P("occ", None, "aux"),
        check_vma=False,
    )
```

```python
import functools
import heapq
import itertools

import jax
import jax.numpy as jnp
from jax import lax
from jax.experimental import pallas as pl
from jax.experimental.pallas import tpu as pltpu
from jax.sharding import PartitionSpec as P

MESH = pl.DeviceIdType.MESH
CORES = 2
GATHER_LIMIT = 24 * 1024 * 1024
LANES = 128
RATE = 46250.0
HOP = 2.6
AHEAD = 2.0
SLACK = 0.0
RETURN = 3.8
ALONE = (2,)
LAST = 0
MIRROR = 2.3
MATMUL = 0.36
ELEMENT = 0.08
APPLY = 0.24
EXCHANGE = 1.4
STEP = {"x": (1, 0, 0), "y": (0, 1, 0), "+": (0, 0, 1), "-": (0, 0, -1)}
BACK = {"x": "x", "y": "y", "+": "-", "-": "+"}
ROUTES = (
    (".xyx+x+++xyy....", ".xyx+++-+++x....", ".xyx+xy++xyy....", ".xyy+-y++xy+...."),
    ("--yy.x+++xyyyy+x", "--yx.xyxx++-++xy", "yx-x.xy++xy-+x+y", "--yx.xyy+xy++xyx"),
)
URGENCY = (4, 1, -1, -2, -1, -2, -1, -1)
DEPTH = 0.5


def from_behind(array, axis, by):
    size = lax.axis_size(axis)
    return lax.ppermute(array, axis, [(i, (i + by) % size) for i in range(size)])


def moved(chip, link):
    dx, dy, dz = STEP[link]
    return ((chip[0] + dx) % 2, (chip[1] + dy) % 2, chip[2] + dz)


def piece_rows(rows):
    number = len(ROUTES[0])
    tiles = rows // 16
    lows = [16 * (tiles * at // number) for at in range(number)] + [rows]
    return [(lows[at], lows[at + 1] - lows[at]) for at in range(number)]


def routes():
    out = []
    for a, b, mirrored in itertools.product(range(2), repeat=3):
        for plane in range(2):
            for piece, text in enumerate(ROUTES[plane]):
                tree = {}
                for z, y, x in itertools.product(range(4), range(2), range(2)):
                    link = text[x + 2 * y + 4 * z]
                    if link == ".":
                        continue
                    px, py, pz = moved((x, y, z), BACK[link])
                    parent = (px ^ a, py ^ b, 3 - pz if mirrored else pz)
                    tree.setdefault(parent, []).append(BACK[link] if mirrored and link in "+-" else link)
                out.append(((a, b, 3 - plane if mirrored else plane), piece, tree))
    return out


def depth_of(tree, chip, known):
    if chip not in known:
        known[chip] = 1 + max([depth_of(tree, moved(chip, link), known) for link in tree.get(chip, ())] or [-1])
    return known[chip]


def timeline(pieces, width):
    items = routes()
    known = [{} for _ in items]
    waiting, busy, arrivals, order, heap = {}, set(), {}, {}, []
    plain = len(items)
    missing = {(x, y, z): 6 * len(pieces) for x, y, z in itertools.product(range(2), range(2), (1, 2))}
    count = itertools.count()
    for at, (source, _, _) in enumerate(items):
        heapq.heappush(heap, (0.0, next(count), True, at, source))

    def start(lane, now):
        if lane in busy or not waiting.get(lane):
            return
        _, _, at, target = heapq.heappop(waiting[lane])
        busy.add(lane)
        taken = pieces[items[at][1]][1] * width * 2 / RATE
        order.setdefault(lane, []).append((now, at))
        heapq.heappush(heap, (now + taken, next(count), False, lane, None))
        heapq.heappush(heap, (now + taken + HOP, next(count), True, at, target))

    while heap:
        now, _, arrived, at, chip = heapq.heappop(heap)
        if not arrived:
            busy.discard(at)
            start(at, now)
            continue
        source, _, tree = items[at]
        arrivals[at, chip] = now
        if at < plain and chip in missing:
            far, near = (3, 0) if chip[2] == 1 else (0, 3)
            if source[2] == far or source[::2] == (chip[0], near):
                missing[chip] -= 1
                ended = missing[chip] == 0
            else:
                ended = False
            if ended:
                for piece in range(len(pieces)):
                    items.append((chip, piece, {chip: ["-" if chip[2] == 1 else "+"]}))
                    known.append({})
                    heapq.heappush(heap, (now + RETURN, next(count), True, len(items) - 1, chip))
        for link in tree.get(chip, ()):
            target = moved(chip, link)
            plane, goal = source[2], target[2]
            if goal >= 2:
                plane, goal = 3 - plane, 3 - goal
            rank = -DEPTH * depth_of(tree, target, known[at]) - URGENCY[2 * plane + goal] if at < plain else LAST
            heapq.heappush(waiting.setdefault((chip, link), []), (rank, next(count), at, target))
            start((chip, link), now)
    return items, arrivals, order, plain


def compute_steps(ready, inner):
    own = 1 if inner else 0
    tasks, jobs = [], []
    work = [("open", 0, 0.0)] + [("matmul", part, MATMUL) for part in range(2)]
    work += [("element", part, ELEMENT) for part in range(4)] + [("mine", 0, APPLY)]

    def add(when, rank, plane, far, dx, extra=()):
        jobs.append((when, rank, len(tasks), work + list(extra)))
        tasks.append((plane, far, dx))

    for plane in sorted({key[0] for key in ready}):
        if inner and plane == 3:
            order = sorted((max(ready[plane, dx], ready[0, 0]), dx) for dx in range(2))
            add(*order[0][:1], 0, plane, True, order[0][1])
            add(*order[1][:1], 0, plane, True, order[1][1], [("return", 0, 0.1)])
        if plane in ALONE:
            for dx in range(2):
                add(max(ready[plane, dx], ready[own, 0]), 2, plane, False, dx)
        else:
            add(max(ready[plane, 0], ready[plane, 1], ready[own, 0]), 2, plane, False, None)
    steps, clock = [], 0.0
    while jobs:
        clock = max(clock, min(job[0] for job in jobs))
        job = min((job for job in jobs if job[0] <= clock), key=lambda job: (job[1], job[0], job[2]))
        kind, part, cost = job[3].pop(0)
        steps.append((clock, kind, job[2], part))
        clock += cost
        if not job[3]:
            jobs.remove(job)
        if kind == "mine" and tasks[job[2]][2] is None:
            jobs.append((clock + EXCHANGE, 1, job[2], [("other", 0, APPLY)]))
    return tasks, steps, clock


def program_of(plane, pieces, width):
    items, arrivals, order, plain = timeline(pieces, width)
    chip = (0, 0, plane)
    events = []
    ready = {}
    for at, (source, piece, _) in enumerate(items[:plain]):
        if (at, chip) in arrivals:
            key = (source[2], source[0])
            ready[key] = max(ready.get(key, 0.0), arrivals[at, chip] + MIRROR)
    tasks, steps, end = compute_steps(ready, plane == 1)
    back = max([when for when, kind, _, _ in steps if kind == "return"] or [0.0])
    first = {}
    for link in STEP:
        last = 0.0
        for when, at in order.get((chip, link), ()):
            last = max(last, arrivals[at, chip], when - AHEAD)
            if at < plain:
                first[at] = min(first.get(at, 1e9), last)
                events.append((last, 2, ("send", items[at][0], items[at][1], link)))
            else:
                events.append((max(last, back + 0.01), 4, ("return", items[at][1])))
    for at, (source, piece, _) in enumerate(items[:plain]):
        if (at, chip) in arrivals:
            when = 1.0 if source == chip else min(arrivals[at, chip] + SLACK, first.get(at, 1e9))
            events.append((when, 1, ("take", source, piece)))
    events += [(when, 3, ("step", *step)) for when, *step in steps]
    for away in range(4 if plane == 1 else 3):
        if away != plane:
            events.append((5.0 * abs(away - plane), 0, ("energy", away)))
    if plane == 0:
        events.append((end + 100.0, 4, ("far",)))
    events.sort(key=lambda event: event[:2])
    return [event[2] for event in events], tasks


def gather_kernel(nz, nx, ny, hbm_ref, occ_ref, row_ref, out_ref, b_ref, e_ref, col_ref, blocks, energies, value, mine_amps, other_amps,
                  total, leave, come, send_sem, recv_sem, msend_sem, mrecv_sem, esend_sem, erecv_sem,
                  asend_sem, arecv_sem, fsend_sem, frecv_sem, keep_sem, load_sem, unused_sem):
    rows, width = b_ref.shape
    occ, aux = lax.axis_index("occ"), lax.axis_index("aux")
    z, x = occ // nx, occ % nx
    y, core = aux // CORES, aux % CORES
    upper = z // 2
    plane = z + upper * (nz - 1 - 2 * z)
    pieces = piece_rows(rows)

    def plane_at(k):
        return k + upper * (nz - 1 - 2 * k)

    def block_at(dx, k):
        return plane_at(k) * nx + (x + dx) % nx

    def device(dx, dy, k, dc=0):
        return block_at(dx, k), ((y + dy) % ny) * CORES + (core + dc) % CORES

    def neighbour(me, link):
        dx, dy, dz = STEP[link]
        return device(dx, dy, me + dz)

    def columns(shard_aux):
        return pl.ds(pl.multiple_of(shard_aux * width, width), width)

    keep = pltpu.make_async_copy(b_ref, blocks.at[occ, :, columns(aux)], keep_sem)
    load = pltpu.make_async_copy(hbm_ref, b_ref, load_sem)
    load.start()
    partner = (occ, y * CORES + (core + 1) % CORES)
    barrier = pltpu.get_barrier_semaphore()
    step_up = 1 - 2 * upper
    near = [
        partner,
        (z * nx + (x + 1) % nx, aux),
        (occ, ((y + 1) % ny) * CORES + core),
        ((z + step_up) * nx + x, aux),
    ]
    for target in near:
        pl.semaphore_signal(barrier, inc=1, device_id=target, device_id_type=MESH)

    @pl.when(plane == 1)
    def _():
        pl.semaphore_signal(barrier, inc=1, device_id=((z - step_up) * nx + x, aux), device_id_type=MESH)

    e_ref[...] = jnp.full(e_ref.shape, occ_ref[0], jnp.float32)
    col_ref[...] = jnp.broadcast_to(row_ref[...], (8, rows)).T[:, 0:1]
    load.wait()
    keep.start()
    pl.semaphore_wait(barrier, len(near) + plane)

    def run(me):
        events, tasks = program_of(me, pieces, width)
        sent = []
        taken = set()
        started = {}

        def place(source, piece, dc=0):
            block, shard_aux = device(source[0], source[1], source[2], dc)
            low, number = pieces[piece]
            return blocks.at[block, pl.ds(low, number), columns(shard_aux)]

        def chip_index(source):
            block, shard_aux = device(*source)
            return block * ny + shard_aux // CORES

        def origin(source, piece):
            low, number = pieces[piece]
            return b_ref.at[pl.ds(low, number)] if source == (0, 0, me) else place(source, piece)

        def remote(src, dst, send, recv, target):
            return pltpu.make_async_remote_copy(
                src_ref=src, dst_ref=dst, send_sem=send, recv_sem=recv, device_id=target, device_id_type=MESH
            )

        def start(copy):
            copy.start()
            sent.append(copy)

        def arrived(spot, sem):
            remote(spot, spot, unused_sem, sem, (occ, aux)).wait_recv()

        for target in ["x", "+"] + (["-"] if me == 1 else []):
            start(remote(e_ref, energies.at[occ], esend_sem.at[len(sent)], erecv_sem.at[occ], neighbour(me, target)))
        number_sent = [0]

        def send(source, piece, link):
            copy = remote(
                origin(source, piece), place(source, piece), send_sem.at[number_sent[0]],
                recv_sem.at[piece, chip_index(source)], neighbour(me, link),
            )
            number_sent[0] += 1
            start(copy)

        def take(source, piece):
            if source != (0, 0, me):
                arrived(place(source, piece), recv_sem.at[piece, chip_index(source)])
            start(remote(
                origin(source, piece), place(source, piece), msend_sem.at[piece, chip_index(source)],
                mrecv_sem.at[piece, chip_index(source)], partner,
            ))

        def pass_energy(away):
            if away in passed:
                return
            passed.add(away)
            block = block_at(0, away)
            arrived(energies.at[block], erecv_sem.at[block])
            onward = ["x"] + ({0: ["+"], 2: ["-"]}.get(away, []) if me == 1 else [])
            for link in onward:
                start(remote(energies.at[block], energies.at[block], esend_sem.at[count_energy[0]],
                             erecv_sem.at[block], neighbour(me, link)))
                count_energy[0] += 1

        count_energy = [len(sent)]
        passed = {me}
        energies[occ] = e_ref[...]

        def open_block(dx, k):
            if (dx, k) in taken:
                return
            taken.add((dx, k))
            if dx == 0:
                pass_energy(k)
            else:
                block = block_at(1, k)
                arrived(energies.at[block], erecv_sem.at[block])
            if (dx, k) == (0, me):
                keep.wait()
            for source in itertools.product([dx], range(2), [k]):
                for piece in range(len(pieces)):
                    arrived(place(source, piece, 1), mrecv_sem.at[piece, chip_index(source)])

        def hand_over(at, part):
            size = -(-rows // (4 * LANES)) * LANES
            low, high = min(part * size, rows), min(part * size + size, rows)
            if high > low:
                spot = pl.ds(low, high - low)
                start(remote(mine_amps.at[at, spot], other_amps.at[at, spot], asend_sem.at[at, part],
                             arecv_sem.at[at, part], partner))

        def apply(amps, block, far, fresh):
            term = jnp.dot(amps, blocks[block, :, columns(aux)], preferred_element_type=jnp.float32)
            goal = total if far else out_ref
            goal[...] = term if fresh else goal[...] + term

        def step(kind, at, part):
            k, far, dx = tasks[at]
            left = block_at(0, 0) if far else occ
            right = plane_at(k) * nx + (x + (core if dx is None else dx)) % nx
            if kind == "open":
                open_block(0, 0 if far else me)
                for which in range(2) if dx is None else [dx]:
                    open_block(which, k)
            elif kind == "matmul":
                cut = rows // 2 // LANES * LANES + LANES if rows > LANES else rows
                low, high = ((0, min(cut, rows)), (min(cut, rows), rows))[part]
                if high > low:
                    value[int(far), :, low:high] = lax.dot_general(
                        blocks[left], blocks[right, low:high, :], (((1,), (1,)), ((), ())),
                        preferred_element_type=jnp.float32,
                    )
            elif kind == "element":
                size = -(-rows // (4 * LANES)) * LANES
                low, high = min(part * size, rows), min(part * size + size, rows)
                if high > low:
                    numer = 2.0 * value[int(far), low:high, :] - value[int(far), :, low:high].T
                    denom = col_ref[low:high, :] + row_ref[...] - energies[left, 0:1, 0:1] - energies[right, 0:1, 0:1]
                    mine_amps[at, low:high, :] = (numer / denom).astype(jnp.bfloat16)
                if part and dx is None:
                    hand_over(at, part - 1)
            elif kind == "mine":
                apply(mine_amps[at], right, far, far not in started)
                started[far] = True
                if dx is None:
                    hand_over(at, 3)
            elif kind == "other":
                size = -(-rows // (4 * LANES)) * LANES
                for piece in range(4):
                    low, high = min(piece * size, rows), min(piece * size + size, rows)
                    if high > low:
                        arrived(other_amps.at[at, pl.ds(low, high - low)], arecv_sem.at[at, piece])
                apply(other_amps[at], plane_at(k) * nx + (x + 1 - core) % nx, far, False)
            elif kind == "return":
                leave[...] = total[...].astype(jnp.bfloat16)

        for event in events:
            if event[0] == "take":
                take(*event[1:])
            elif event[0] == "send":
                send(*event[1:])
            elif event[0] == "energy":
                pass_energy(event[1])
            elif event[0] == "step":
                step(*event[1:])
            elif event[0] == "return":
                spot = pl.ds(*pieces[event[1]])
                start(remote(leave.at[spot], come.at[spot], fsend_sem.at[event[1]], frecv_sem.at[event[1]],
                             neighbour(me, "-")))
            else:
                for piece, (low, number) in enumerate(pieces):
                    spot = slice(low, low + number)
                    arrived(come.at[pl.ds(low, number)], frecv_sem.at[piece])
                    out_ref[spot, :] = out_ref[spot, :] + come[spot, :].astype(jnp.float32)
        for copy in sent:
            copy.wait_send()

    @pl.when(plane == 0)
    def _():
        run(0)

    @pl.when(plane == 1)
    def _():
        run(1)


def gathered(three_index, occ_energy, vir_energy, nz, nx, ny):
    _, rows, width = three_index.shape
    nocc, naux = nz * nx, ny * CORES
    pieces = piece_rows(rows)
    copies = max(sum(event[0] == "send" for event in program_of(plane, pieces, width)[0]) for plane in range(2))
    tasks = max(len(program_of(plane, pieces, width)[1]) for plane in range(2))
    vmem = pl.BlockSpec(memory_space=pltpu.VMEM)
    dma = pltpu.SemaphoreType.DMA
    kind = three_index.dtype
    out = pl.pallas_call(
        functools.partial(gather_kernel, nz, nx, ny),
        out_shape=jax.ShapeDtypeStruct((rows, width), jnp.float32),
        in_specs=[pl.BlockSpec(memory_space=pltpu.HBM), pl.BlockSpec(memory_space=pltpu.SMEM), vmem],
        out_specs=vmem,
        scratch_shapes=[
            pltpu.VMEM((rows, width), kind),
            pltpu.VMEM((8, LANES), jnp.float32),
            pltpu.VMEM((rows, 1), jnp.float32),
            pltpu.VMEM((nocc, rows, naux * width), kind),
            pltpu.VMEM((nocc, 8, LANES), jnp.float32),
            pltpu.VMEM((2, rows, rows), jnp.float32),
            pltpu.VMEM((tasks, rows, rows), jnp.bfloat16),
            pltpu.VMEM((tasks, rows, rows), jnp.bfloat16),
            pltpu.VMEM((rows, width), jnp.float32),
            pltpu.VMEM((rows, width), jnp.bfloat16),
            pltpu.VMEM((rows, width), jnp.bfloat16),
            dma((copies,)),
            dma((len(pieces), nocc * ny)),
            dma((len(pieces), nocc * ny)),
            dma((len(pieces), nocc * ny)),
            dma((16,)),
            dma((nocc,)),
            dma((tasks, 4)),
            dma((tasks, 4)),
            dma((len(pieces),)),
            dma((len(pieces),)),
            dma,
            dma,
            dma,
        ],
        compiler_params=pltpu.CompilerParams(
            collective_id=0, has_side_effects=True, vmem_limit_bytes=48 * 1024 * 1024
        ),
    )(three_index[0], occ_energy, vir_energy[None, :])
    return out[None]


def pair_amps(rows_i, eps_i, rows_j, eps_j, vir_energy):
    partial_value = lax.dot_general(
        rows_i, rows_j, (((1,), (1,)), ((), ())), preferred_element_type=jnp.float32
    )
    occ_count = eps_i.shape[0]
    vir_count = vir_energy.shape[0]
    width = occ_count * vir_count
    four = partial_value.reshape(occ_count, vir_count, occ_count, vir_count)
    numer = (2.0 * four - jnp.transpose(four, (0, 3, 2, 1))).reshape(width, width)
    denom = (
        vir_energy[None, :, None, None]
        + vir_energy[None, None, None, :]
        - eps_i[:, None, None, None]
        - eps_j[None, None, :, None]
    ).reshape(width, width)
    share = width // lax.axis_size("aux")
    mine = lax.psum_scatter(numer, "aux", scatter_dimension=0, tiled=True)
    lower = lax.axis_index("aux") * share
    denom_rows = lax.dynamic_slice_in_dim(denom, lower, share, 0)
    amps_rows = (mine / denom_rows).astype(jnp.bfloat16)
    amps = lax.all_gather(amps_rows, "aux", axis=0, tiled=True)
    return amps


def apply_other(amps, rows_i):
    return lax.dot_general(
        amps, rows_i, (((0,), (0,)), ((), ())), preferred_element_type=jnp.float32
    )


def local(three_index, occ_energy, vir_energy):
    occ_count, vir_count, aux_count = three_index.shape
    cycle_size = lax.axis_size("occ")
    my_index = lax.axis_index("occ")
    all_energy = lax.all_gather(occ_energy, "occ", axis=0, tiled=True)
    own_rows = three_index.reshape(occ_count * vir_count, aux_count)

    def energy_of(step):
        block = (my_index - step + cycle_size) % cycle_size
        return lax.dynamic_slice_in_dim(all_energy, block * occ_count, occ_count)

    amps = pair_amps(own_rows, occ_energy, own_rows, occ_energy, vir_energy)
    gamma = jnp.dot(amps, own_rows, preferred_element_type=jnp.float32)
    half = cycle_size // 2
    carried = jnp.zeros_like(gamma)

    def cycle_step(step, state):
        rows_j, carried, gamma = state
        rows_j = from_behind(rows_j, "occ", 1)
        carried = from_behind(carried, "occ", 1)
        amps = pair_amps(own_rows, occ_energy, rows_j, energy_of(step), vir_energy)
        gamma = gamma + jnp.dot(amps, rows_j, preferred_element_type=jnp.float32)
        carried = carried + apply_other(amps, own_rows)
        return (rows_j, carried, gamma)

    rows_j, carried, gamma = lax.fori_loop(1, half, cycle_step, (own_rows, carried, gamma))
    rows_j = from_behind(rows_j, "occ", 1)
    amps = pair_amps(own_rows, occ_energy, rows_j, energy_of(half), vir_energy)
    gamma = gamma + jnp.dot(amps, rows_j, preferred_element_type=jnp.float32)
    returned = from_behind(carried, "occ", 1 - half)
    gamma = gamma + returned
    return gamma.reshape(occ_count, vir_count, aux_count)


def solution(mesh):
    nocc, naux = mesh.shape["occ"], mesh.shape["aux"]

    def either(three_index, occ_energy, vir_energy):
        _, rows, width = three_index.shape
        whole = nocc * naux * three_index.size * three_index.dtype.itemsize
        pieces = len(ROUTES[0])
        fits = whole <= GATHER_LIMIT and three_index.shape[0] == 1
        fits = fits and rows % 16 == 0 and rows // 16 >= pieces and width % LANES == 0
        if fits and nocc == 8 and naux == 2 * CORES:
            return gathered(three_index, occ_energy, vir_energy, nocc // 2, 2, naux // CORES)
        return local(three_index, occ_energy, vir_energy)

    return jax.shard_map(
        either,
        mesh=mesh,
        in_specs=(P("occ", None, "aux"), P("occ"), P()),
        out_specs=P("occ", None, "aux"),
        check_vma=False,
    )
```
